512 devices in a mesh: ctx: 64 (over y, z), tp: 8 (over x, core).
Axes of the slice: x: 4, y: 4, z: 16, core: 2. Of those that a mesh axis runs over, the one named last changes fastest.
Arguments:
- queries: bfloat16 [8192, 4096], P('ctx', 'tp'), may hold values from -16 to 16
- keys: bfloat16 [8192, 1024], P('ctx', 'tp'), may hold values from -7.1 to 7.1
- values: bfloat16 [8192, 1024], P('ctx', 'tp'), may hold values from -6 to 6
- mixer_input: bfloat16 [8192, 8192], P('ctx', 'tp'), may hold values from -6 to 6
- gate: bfloat16 [8192, 8192], P('ctx', 'tp'), may hold values from -6 to 6
- step_weight: bfloat16 [8192, 128], P('tp'), may hold values from -0.0625 to 0.0625
- state_weight: bfloat16 [8192, 32], P('tp'), may hold values from -0.0625 to 0.0625
- step_bias: float32 [128], P('tp'), may hold values from -1 to 1
- decay_rate: float32 [128], P('tp'), may hold values from 1.2207031e-06 to 0.05
- skip_gain: float32 [128], P('tp'), may hold values from 0.5 to 2
- norm_gain: float32 [8192], P('tp'), may hold values from 0.1 to 1.9
Outputs:
- attention_out: bfloat16 [8192, 4096], P('ctx', 'tp')
- mamba_out: bfloat16 [8192, 8192], P('ctx', 'tp')
The draws below stay inside these ranges and needn't reach their ends.
All inputs are finite; a program needn't handle non-finite values.
Results may differ from the reference program's by a relative error of at most 0.0044.
Values may be sent and summed in bfloat16 or wider, within the bound.
A program may use at most 64 MiB of HBM per device.

```python
import math
import jax
import jax.numpy as jnp
from jax import lax

QHEADS = 32
KVHEADS = 8
HD = 128
INNER_CHANNELS = 8192
STATE_WIDTH = 16
DECAY_CHANNELS = 64
SCAN_TOKENS = 128
TOK_DEV = 128
TOKENS = 8192
MHEADS = 128


def draw_keys(key, part):
    noise = jax.random.normal(jax.random.fold_in(key, 13), (TOKENS, KVHEADS, HD), jnp.float32)
    noise = jnp.clip(noise, -6.0, 6.0)
    return noise.reshape(TOKENS, KVHEADS * HD).astype(jnp.bfloat16)


def draw_queries(key, part):
    noise = jax.random.normal(jax.random.fold_in(key, 11), (TOKENS, QHEADS, HD), jnp.float32)
    noise = jnp.clip(noise, -6.0, 6.0)
    return noise.reshape(TOKENS, QHEADS * HD).astype(jnp.bfloat16)


def level_of(own_key, shape, shards, low, high):
    gain = 1.0
    for position, parts in shards:
        heights = jax.random.uniform(jax.random.fold_in(jax.random.fold_in(own_key, 6), position), (parts,), jnp.float32, low / len(shards), high / len(shards))
        gain = gain * jnp.repeat(jnp.exp(heights), shape[position] // parts).reshape((-1,) + (1,) * (len(shape) - 1 - position))
    return gain


def bell_draw(stream_key, shape, spread, most, pieces=(), held_as=jnp.bfloat16):
    values = spread * jax.random.normal(stream_key, shape, jnp.float32)
    if pieces:
        values = values * level_of(stream_key, shape, pieces, -0.22, 0.18)
    return jnp.clip(values, -most, most).astype(held_as)


def setup_inputs(seed: int = 0) -> dict:
    arg_keys = jax.random.split(jax.random.key(seed), 12)
    queries = draw_queries(jax.random.fold_in(arg_keys[11], 71), 0)
    keys = draw_keys(jax.random.fold_in(arg_keys[11], 71), 0)
    values = bell_draw(arg_keys[2], (TOKENS, KVHEADS * HD), 1.0, 6.0, ((0, 64), (1, 8)))
    mixer_input = bell_draw(arg_keys[3], (TOKENS, INNER_CHANNELS), 1.0, 6.0, ((0, 64), (1, 8)))
    gate = bell_draw(arg_keys[4], (TOKENS, INNER_CHANNELS), 1.0, 6.0, ((0, 64), (1, 8)))
    step_weight = bell_draw(arg_keys[5], (INNER_CHANNELS, MHEADS), INNER_CHANNELS ** -0.5, 0.0625, ((0, 8),))
    state_weight = bell_draw(arg_keys[6], (INNER_CHANNELS, 2 * STATE_WIDTH), INNER_CHANNELS ** -0.5, 0.0625, ((0, 8),))
    step_bias = jnp.clip(jax.random.uniform(arg_keys[7], (MHEADS,), jnp.float32, -1.0, 1.0) * level_of(arg_keys[7], (MHEADS,), ((0, 8),), -0.4, 0.0), -1.0, 1.0)
    decay_rate = jnp.clip(jnp.exp(math.log(0.05) - 10.620351 * jax.random.uniform(arg_keys[8], (MHEADS,), jnp.float32) ** level_of(arg_keys[8], (MHEADS,), ((0, 8),), -0.2, 0.2)), 1.220703097715159e-06, 0.05)
    skip_gain = jnp.clip(jnp.exp(math.log(2.0) - 1.3862944 * jax.random.uniform(arg_keys[9], (MHEADS,), jnp.float32) ** level_of(arg_keys[9], (MHEADS,), ((0, 8),), -0.2, 0.2)), 0.5, 2.0)
    norm_gain = jnp.clip(1.0 + 0.18 * jax.random.normal(arg_keys[10], (INNER_CHANNELS,), jnp.float32), 0.1, 1.9)
    return {"queries": queries, "keys": keys, "values": values, "mixer_input": mixer_input, "gate": gate, "step_weight": step_weight, "state_weight": state_weight, "step_bias": step_bias, "decay_rate": decay_rate, "skip_gain": skip_gain, "norm_gain": norm_gain}


def attention(queries, keys, values):
    group = QHEADS // KVHEADS
    scale = 1.0 / math.sqrt(HD)
    keys_wide = keys.reshape(TOKENS, KVHEADS, HD).astype(jnp.float32)
    values_wide = values.reshape(TOKENS, KVHEADS, HD).astype(jnp.float32)
    block = TOK_DEV // 2
    block_count = TOKENS // block
    key_positions = jnp.arange(TOKENS, dtype=jnp.int32)

    def one_block(number):
        first = number * block
        rows = lax.dynamic_slice_in_dim(queries, first, block, 0)
        rows = rows.reshape(block, KVHEADS, group, HD).astype(jnp.float32)
        scores = jnp.einsum('tkgd,skd->kgts', rows, keys_wide) * scale
        query_positions = first + jnp.arange(block, dtype=jnp.int32)
        mask = key_positions[None, :] <= query_positions[:, None]
        scores = jnp.where(mask, scores, -1e+30)
        row_max = lax.optimization_barrier(jnp.max(scores, axis=-1, keepdims=True))
        expos = jnp.where(mask, jnp.exp(scores - row_max), 0.0)
        total = lax.optimization_barrier(jnp.sum(expos, axis=-1))
        weights = lax.optimization_barrier(expos.astype(jnp.bfloat16)).astype(jnp.float32)
        mixed = jnp.einsum('kgts,skd->tkgd', weights, values_wide)
        mixed = mixed / jnp.transpose(total, (2, 0, 1))[..., None]
        return mixed.reshape(block, QHEADS * HD).astype(jnp.bfloat16)
    outputs = lax.map(one_block, jnp.arange(block_count, dtype=jnp.int32))
    return outputs.reshape(TOKENS, QHEADS * HD)

def mixer(mixer_input, gate, step_weight, state_weight, step_bias, decay_rate, skip_gain, norm_gain):
    head_count = INNER_CHANNELS // DECAY_CHANNELS
    step_raw = jnp.dot(mixer_input, step_weight, preferred_element_type=jnp.float32)
    maps = jnp.dot(mixer_input, state_weight, preferred_element_type=jnp.float32)
    step = jax.nn.softplus(step_raw + step_bias)
    log_decay = -decay_rate * step
    block_count = TOKENS // SCAN_TOKENS
    decay_blocks = log_decay.reshape(block_count, SCAN_TOKENS, head_count)
    step_blocks = step.reshape(block_count, SCAN_TOKENS, head_count)
    b_rows = maps[:, :STATE_WIDTH].reshape(block_count, SCAN_TOKENS, STATE_WIDTH)
    c_rows = maps[:, STATE_WIDTH:].reshape(block_count, SCAN_TOKENS, STATE_WIDTH)
    input_blocks = mixer_input.reshape(block_count, SCAN_TOKENS, head_count, DECAY_CHANNELS)
    causal = jnp.arange(SCAN_TOKENS)[:, None] >= jnp.arange(SCAN_TOKENS)[None, :]

    def one_block(carry, items):
        decay_here, step_here, b_here, c_here, x_here = items
        climb = jnp.cumsum(decay_here, axis=0)
        inner = jnp.dot(c_here, b_here.T, precision=lax.Precision.HIGHEST, preferred_element_type=jnp.float32)
        climb_t = climb.T
        diff = climb_t[:, :, None] - climb_t[:, None, :]
        decay = jnp.where(causal[None], jnp.exp(jnp.where(causal[None], diff, 0.0)), 0.0)
        mix = (inner[None] * decay * step_here.T[:, None, :]).astype(jnp.bfloat16)
        mix_wide = lax.optimization_barrier(mix).astype(jnp.float32)
        x_wide = x_here.astype(jnp.float32)
        local = jnp.einsum('hts,shp->thp', mix_wide, x_wide)
        carried = jnp.exp(climb)[:, :, None] * jnp.einsum('tn,nhp->thp', c_here, carry, precision=lax.Precision.HIGHEST)
        y_block = local + carried + skip_gain[None, :, None] * x_wide
        final = climb[-1]
        feed = (b_here[:, :, None] * (jnp.exp(final[None, :] - climb) * step_here)[:, None, :]).astype(jnp.bfloat16)
        feed_wide = lax.optimization_barrier(feed).astype(jnp.float32)
        new_carry = jnp.exp(final)[None, :, None] * carry + jnp.einsum('snh,shp->nhp', feed_wide, x_wide)
        return (new_carry, y_block)
    start_index = jnp.zeros((STATE_WIDTH, head_count, DECAY_CHANNELS), jnp.float32)
    ending, y_all = lax.scan(one_block, start_index, (decay_blocks, step_blocks, b_rows, c_rows, input_blocks))
    y_flat = y_all.reshape(TOKENS, INNER_CHANNELS)
    gated = y_flat * jax.nn.silu(gate.astype(jnp.float32))
    mean_square = lax.optimization_barrier(jnp.mean(gated * gated, axis=-1, keepdims=True))
    normed = gated * lax.rsqrt(mean_square + 1e-05)
    return (normed * norm_gain).astype(jnp.bfloat16)

def reference(queries, keys, values, mixer_input, gate, step_weight, state_weight, step_bias, decay_rate, skip_gain, norm_gain):
    attention_out = attention(queries, keys, values)
    mamba_out = mixer(mixer_input, gate, step_weight, state_weight, step_bias, decay_rate, skip_gain, norm_gain)
    return (attention_out, mamba_out)
```

```python
import functools
import math

import jax
import jax.numpy as jnp
from jax import lax
from jax.experimental import pallas as pl
from jax.experimental.pallas import tpu as pltpu
from jax.sharding import PartitionSpec as P

HD = 128
TOK = 128
ROW = 16
ROWS = 4
TP = 8
HEADS = 16
STATE = 16
PAIRS = 8
CHANNELS = 8192
SCALE = 1.0 / math.sqrt(HD)
F32 = jnp.float32
BF16 = jnp.bfloat16
EXACT = lax.Precision.HIGHEST
MESH = pl.DeviceIdType.MESH


def dot(a, b, precision=None):
    return jnp.dot(a, b, preferred_element_type=F32, precision=precision)


def dot_t(a, b, precision=None):
    return lax.dot_general(
        a, b, (((1,), (1,)), ((), ())), preferred_element_type=F32, precision=precision
    )


def kernel(
    q_ref, k_ref, v_ref, x_ref, gate_ref, ws_ref, wm_ref, bias_ref, rate_ref, skip_ref, norm_ref,
    attn_ref, mamba_ref,
    kbuf, vbuf, qbuf, obuf, orecv, stat_send, stat_recv, own_out, acc_out,
    proj_send, proj_recv, csend, crecv, fsend, frecv, ysend, yrecv, rsend, srecv,
    base, gated, sqsend, sqrecv, pref,
    ring_ss, ring_rs, q_ss, q_rs, o_ss, o_rs, st_ss, st_rs, grp_ss, grp_rs,
):
    me = lax.axis_index("ctx")
    t = lax.axis_index("tp")
    y, z = me // ROW, me % ROW

    def tp_peer(o):
        return lax.rem(t + o, TP)

    def z_peer(o):
        return y * ROW + lax.rem(z + o + ROW, ROW)

    def y_peer(o):
        return lax.rem(y + o + ROWS, ROWS) * ROW + z

    def at(ctx, tp):
        return {"ctx": ctx, "tp": tp}

    barrier = pltpu.get_barrier_semaphore()
    for o in range(1, TP):
        pl.semaphore_signal(barrier, inc=1, device_id=at(me, tp_peer(o)), device_id_type=MESH)
    for o in range(1, ROW):
        pl.semaphore_signal(barrier, inc=1, device_id=at(z_peer(o), t), device_id_type=MESH)
    for o in range(1, ROWS):
        pl.semaphore_signal(barrier, inc=1, device_id=at(y_peer(o), t), device_id_type=MESH)

    ws = dot(x_ref[...], ws_ref[...])
    wm = dot(x_ref[...], wm_ref[...])
    step_part = ws.T
    maps_part = jnp.concatenate([wm, jnp.zeros((TOK, 96), F32)], axis=1).T[:32]
    for p in range(TP):
        proj_send[p, 0:16, :] = step_part[16 * p:16 * p + 16]
        proj_send[p, 16:48, :] = maps_part
    kbuf[z] = k_ref[...]
    vbuf[z] = v_ref[...]

    pl.semaphore_wait(barrier, TP - 1 + ROW - 1 + ROWS - 1)

    def remote(src, dst, ssem, rsem, ctx, tp):
        return pltpu.make_async_remote_copy(
            src_ref=src, dst_ref=dst, send_sem=ssem, recv_sem=rsem,
            device_id=at(ctx, tp), device_id_type=MESH,
        )

    def proj_copy(o):
        return remote(
            proj_send.at[tp_peer(o)], proj_recv.at[t], grp_ss.at[0], grp_rs.at[0], me, tp_peer(o)
        )

    for o in range(1, TP):
        proj_copy(o).start()

    def ring_copy(kv, d, s):
        block = lax.rem(z - d * (s - 1) + 2 * ROW, ROW)
        buf = (kbuf, vbuf)[kv]
        i = 0 if d > 0 else 1
        src = (k_ref, v_ref)[kv] if s == 1 else buf.at[block]
        return remote(
            src, buf.at[block], ring_ss.at[kv, i, s - 1], ring_rs.at[kv, i, s - 1], z_peer(d), t
        )

    def ring_steps(d):
        return ROW // 2 if d > 0 else ROW // 2 - 1

    for kv in (0, 1):
        for d in (1, -1):
            ring_copy(kv, d, 1).start()

    def ring(s):
        for kv in (0, 1):
            for d in (1, -1):
                if s <= ring_steps(d):
                    ring_copy(kv, d, s).wait_recv()
                    if s + 1 <= ring_steps(d):
                        ring_copy(kv, d, s + 1).start()

    def q_copy(o):
        return remote(q_ref, qbuf.at[o - 1], q_ss.at[o - 1], q_rs.at[o - 1], y_peer(-o), t)

    for o in range(1, ROWS):
        @pl.when(y >= o)
        def _(o=o):
            q_copy(o).start()

    lane = lax.broadcasted_iota(jnp.int32, (TOK, TOK), 1)
    sub = lax.broadcasted_iota(jnp.int32, (TOK, TOK), 0)
    low = lane < 64
    sub16 = lax.broadcasted_iota(jnp.int32, (HEADS, TOK), 0)
    lane16 = lax.broadcasted_iota(jnp.int32, (HEADS, TOK), 1)

    def column(ref):
        out = jnp.full((HEADS, TOK), ref[0], F32)
        for h in range(1, HEADS):
            out = jnp.where(sub16 == h, ref[h], out)
        return out

    bias, rate = column(bias_ref), column(rate_ref)
    ring(1)

    remote(
        proj_send.at[0:TP - 1], proj_recv.at[0:TP - 1], grp_ss.at[0], grp_rs.at[0], me, tp_peer(1)
    ).wait_recv()
    proj_recv[t] = proj_send[t]
    total = proj_recv[0]
    for p in range(1, TP):
        total = total + proj_recv[p]
    b_rows, c_rows = total[16:32], total[32:48]
    raw = total[0:16] + bias
    step = jnp.maximum(raw, 0.0) + jnp.log1p(jnp.exp(-jnp.abs(raw)))
    climb = -rate * step
    for sh in (1, 2, 4, 8, 16, 32, 64):
        climb = climb + jnp.where(lane16 >= sh, pltpu.roll(climb, sh, axis=1), 0.0)
    final = jnp.broadcast_to(climb[:, TOK - 1:TOK], (HEADS, TOK))
    for j in range(PAIRS):
        fsend[j] = jnp.where(low[0:1], final[2 * j:2 * j + 1], final[2 * j + 1:2 * j + 2])
    def f_copy(o):
        return remote(
            fsend.at[lax.rem(z + o, ROW) // 2], frecv.at[z], grp_ss.at[1], grp_rs.at[1],
            z_peer(o), t,
        )

    for o in range(1, ROW):
        f_copy(o).start()
    feed_weight = jnp.exp(final - climb) * step

    def pair_input(j):
        xp = x_ref[:, 128 * j:128 * j + 128]
        zero = jnp.zeros_like(xp)
        return jnp.concatenate([jnp.where(low, xp, zero), jnp.where(low, zero, xp)], axis=0)

    for j in range(PAIRS):
        feed = jnp.concatenate(
            [b_rows * feed_weight[h:h + 1] for h in (2 * j, 2 * j + 1)], axis=1
        ).astype(BF16)
        contrib = dot(feed, pair_input(j))
        csend[2 * j] = contrib[0:8]
        csend[2 * j + 1] = contrib[8:16]

    def c_copy(o):
        return remote(
            csend.at[lax.rem(z + o, ROW)], crecv.at[z], grp_ss.at[2], grp_rs.at[2], z_peer(o), t
        )

    for o in range(1, ROW):
        c_copy(o).start()
    crecv[z] = csend[z]
    frecv[z] = fsend[z // 2]
    ring(2)

    turned = jnp.concatenate([c_rows, climb, jnp.exp(climb), jnp.zeros((80, TOK), F32)], axis=0).T
    c_cols = turned[:, 0:16]
    inner = dot(c_cols, b_rows, EXACT)
    causal = sub >= lane

    def local_pair(j):
        mixes = []
        for h in (2 * j, 2 * j + 1):
            diff = turned[:, 16 + h:17 + h] - climb[h:h + 1]
            mix = inner * jnp.exp(diff) * step[h:h + 1]
            mixes.append(jnp.where(causal, mix, 0.0).astype(BF16))
        out = dot(jnp.concatenate(mixes, axis=1), pair_input(j))
        gain = jnp.where(low, skip_ref[2 * j], skip_ref[2 * j + 1])
        cols = slice(128 * j, 128 * j + 128)
        base[:, cols] = out + gain * x_ref[:, cols].astype(F32)

    for j in range(4):
        local_pair(j)
    ring(3)
    for j in range(4, PAIRS):
        local_pair(j)
    ring(4)
    ring(5)

    remote(
        csend.at[0:ROW - 1], crecv.at[0:ROW - 1], grp_ss.at[2], grp_rs.at[2], z_peer(1), t
    ).wait_recv()
    remote(
        frecv.at[0:ROW - 1], frecv.at[0:ROW - 1], grp_ss.at[1], grp_rs.at[1], z_peer(1), t
    ).wait_recv()
    running = jnp.zeros((8, TOK), F32)
    passed = jnp.zeros((1, TOK), F32)
    gone = []
    for b in range(ROW):
        pref[b] = running
        gone.append(passed)
        running = jnp.exp(frecv[b]) * running + crecv[b]
        passed = passed + frecv[b]
    ysend[0:8] = running
    ysend[8:16] = jnp.broadcast_to(passed, (8, TOK))

    def y_copy(o):
        return remote(ysend, yrecv.at[y], grp_ss.at[3], grp_rs.at[3], y_peer(o), t)

    for o in range(1, ROWS):
        y_copy(o).start()
    yrecv[y] = ysend[...]
    ring(6)
    remote(
        yrecv.at[0:ROWS - 1], yrecv.at[0:ROWS - 1], grp_ss.at[3], grp_rs.at[3], y_peer(1), t
    ).wait_recv()
    enter = jnp.zeros((8, TOK), F32)
    for r in range(ROWS - 1):
        longer = jnp.exp(yrecv[r, 8:16]) * enter + yrecv[r, 0:8]
        enter = jnp.where(r < y, longer, enter)
    for b in range(ROW):
        rsend[b] = pref[b] + jnp.exp(gone[b]) * enter

    def r_copy(o):
        return remote(
            rsend.at[lax.rem(z + o, ROW)], srecv.at[z], grp_ss.at[4], grp_rs.at[4], z_peer(o), t
        )

    for o in range(1, ROW):
        r_copy(o).start()
    srecv[z] = rsend[z]
    ring(7)
    ring(8)

    keys = ROW * TOK

    def unit(q, masked):
        scores = dot_t(q, kbuf[...].reshape(keys, HD)) * SCALE
        if masked:
            key = lax.broadcasted_iota(jnp.int32, (TOK, keys), 1)
            query = lax.broadcasted_iota(jnp.int32, (TOK, keys), 0) + z * TOK
            mask = key <= query
            scores = jnp.where(mask, scores, -1e30)
        top = jnp.max(scores, axis=1, keepdims=True)
        weights = jnp.exp(scores - top)
        if masked:
            weights = jnp.where(mask, weights, 0.0)
        whole = jnp.sum(weights, axis=1, keepdims=True)
        mixed = dot(weights.astype(BF16), vbuf[...].reshape(keys, HD))
        return mixed / whole, top, whole

    def stats_of(tops, wholes):
        out = jnp.zeros((TOK, TOK), F32)
        for i, col in enumerate(tops + wholes):
            out = jnp.where(lane == i, col, out)
        return out

    def o_copy(o, h):
        cols = slice(128 * h, 128 * h + 128)
        return remote(
            obuf.at[o - 1, h], orecv.at[o - 1, h],
            o_ss.at[o - 1, h], o_rs.at[o - 1, h], y_peer(o), t,
        )

    def st_copy(o):
        return remote(
            stat_send.at[o - 1], stat_recv.at[o - 1], st_ss.at[o - 1], st_rs.at[o - 1],
            y_peer(o), t,
        )

    for o in (3, 2, 1):
        @pl.when(y + o < ROWS)
        def _(o=o):
            q_copy(o).wait_recv()
            tops, wholes = [], []
            for h in range(4):
                mixed, top, whole = unit(qbuf[o - 1, :, 128 * h:128 * h + 128], False)
                obuf[o - 1, h] = mixed.astype(BF16)
                o_copy(o, h).start()
                tops.append(top)
                wholes.append(whole)
            stat_send[o - 1] = stats_of(tops, wholes).T[0:8]
            st_copy(o).start()

    tops, wholes = [], []
    for h in range(4):
        mixed, top, whole = unit(q_ref[:, 128 * h:128 * h + 128], True)
        acc_out[:, 128 * h:128 * h + 128] = mixed
        tops.append(top)
        wholes.append(whole)
    own_out[...] = stats_of(tops, wholes)

    remote(
        rsend.at[0:ROW - 1], srecv.at[0:ROW - 1], grp_ss.at[4], grp_rs.at[4], z_peer(1), t
    ).wait_recv()
    squares = jnp.zeros((TOK, TOK), F32)
    for j in range(PAIRS):
        cols = slice(128 * j, 128 * j + 128)
        state = srecv[2 * j:2 * j + 2].reshape(STATE, TOK)
        grown = jnp.where(low, turned[:, 32 + 2 * j:33 + 2 * j], turned[:, 33 + 2 * j:34 + 2 * j])
        out = base[:, cols] + grown * dot(c_cols, state, EXACT)
        g = gate_ref[:, cols].astype(F32)
        out = out * (g / (1.0 + jnp.exp(-g)))
        gated[:, cols] = out
        squares = squares + out * out
    sqsend[...] = dot_t(jnp.ones((8, TOK), F32), squares, EXACT)

    def sq_copy(o):
        return remote(sqsend, sqrecv.at[t], grp_ss.at[5], grp_rs.at[5], me, tp_peer(o))

    for o in range(1, TP):
        sq_copy(o).start()
    sqrecv[t] = sqsend[...]

    for o in range(1, ROWS):
        @pl.when(y >= o)
        def _(o=o):
            st_copy(o).wait_recv()
            other = jnp.concatenate([stat_recv[o - 1], jnp.zeros((120, TOK), F32)], axis=0).T
            mine = own_out[...]
            tops, wholes = [], []
            for h in range(4):
                o_copy(o, h).wait_recv()
                cols = slice(128 * h, 128 * h + 128)
                top_a, top_b = mine[:, h:h + 1], other[:, h:h + 1]
                top = jnp.maximum(top_a, top_b)
                part_a = mine[:, 4 + h:5 + h] * jnp.exp(top_a - top)
                part_b = other[:, 4 + h:5 + h] * jnp.exp(top_b - top)
                whole = part_a + part_b
                acc_out[:, cols] = (
                    acc_out[:, cols] * (part_a / whole)
                    + orecv[o - 1, h].astype(F32) * (part_b / whole)
                )
                tops.append(top)
                wholes.append(whole)
            own_out[...] = stats_of(tops, wholes)

    attn_ref[...] = acc_out[...].astype(BF16)

    remote(
        sqrecv.at[0:TP - 1], sqrecv.at[0:TP - 1], grp_ss.at[5], grp_rs.at[5], me, tp_peer(1)
    ).wait_recv()
    square = sqrecv[0]
    for p in range(1, TP):
        square = square + sqrecv[p]
    inverse = lax.rsqrt(square[0:1] / CHANNELS + 1e-5)
    inverse = jnp.broadcast_to(inverse, (TOK, TOK)).T
    for j in range(PAIRS):
        cols = slice(128 * j, 128 * j + 128)
        mamba_ref[:, cols] = (gated[:, cols] * inverse * norm_ref[0:1, cols]).astype(BF16)

    remote(
        proj_send.at[0:TP - 1], proj_recv.at[0:TP - 1], grp_ss.at[0], grp_rs.at[0], me, tp_peer(1)
    ).wait_send()
    remote(
        frecv.at[0:ROW - 1], frecv.at[0:ROW - 1], grp_ss.at[1], grp_rs.at[1], z_peer(1), t
    ).wait_send()
    remote(
        csend.at[0:ROW - 1], crecv.at[0:ROW - 1], grp_ss.at[2], grp_rs.at[2], z_peer(1), t
    ).wait_send()
    remote(
        yrecv.at[0:ROWS - 1], yrecv.at[0:ROWS - 1], grp_ss.at[3], grp_rs.at[3], y_peer(1), t
    ).wait_send()
    remote(
        rsend.at[0:ROW - 1], srecv.at[0:ROW - 1], grp_ss.at[4], grp_rs.at[4], z_peer(1), t
    ).wait_send()
    remote(
        sqrecv.at[0:TP - 1], sqrecv.at[0:TP - 1], grp_ss.at[5], grp_rs.at[5], me, tp_peer(1)
    ).wait_send()
    for kv in (0, 1):
        for d in (1, -1):
            for s in range(1, ring_steps(d) + 1):
                ring_copy(kv, d, s).wait_send()
    for o in range(1, ROWS):
        @pl.when(y >= o)
        def _(o=o):
            q_copy(o).wait_send()

        @pl.when(y + o < ROWS)
        def _(o=o):
            for h in range(4):
                o_copy(o, h).wait_send()
            st_copy(o).wait_send()


def per_device(
    queries, keys, values, mixer_input, gate, step_weight, state_weight, step_bias, decay_rate,
    skip_gain, norm_gain,
):
    vmem = pl.BlockSpec(memory_space=pltpu.VMEM)
    smem = pl.BlockSpec(memory_space=pltpu.SMEM)
    return pl.pallas_call(
        kernel,
        out_shape=(
            jax.ShapeDtypeStruct((TOK, 4 * HD), BF16),
            jax.ShapeDtypeStruct((TOK, 1024), BF16),
        ),
        in_specs=[vmem] * 7 + [smem] * 3 + [vmem],
        out_specs=(vmem, vmem),
        scratch_shapes=[
            pltpu.VMEM((ROW, TOK, HD), BF16),
            pltpu.VMEM((ROW, TOK, HD), BF16),
            pltpu.VMEM((3, TOK, 4 * HD), BF16),
            pltpu.VMEM((3, 4, TOK, HD), BF16),
            pltpu.VMEM((3, 4, TOK, HD), BF16),
            pltpu.VMEM((3, 8, TOK), F32),
            pltpu.VMEM((3, 8, TOK), F32),
            pltpu.VMEM((TOK, TOK), F32),
            pltpu.VMEM((TOK, 4 * HD), F32),
            pltpu.VMEM((TP, 48, TOK), F32),
            pltpu.VMEM((TP, 48, TOK), F32),
            pltpu.VMEM((ROW, 8, TOK), F32),
            pltpu.VMEM((ROW, 8, TOK), F32),
            pltpu.VMEM((PAIRS, 1, TOK), F32),
            pltpu.VMEM((ROW, 1, TOK), F32),
            pltpu.VMEM((16, TOK), F32),
            pltpu.VMEM((ROWS, 16, TOK), F32),
            pltpu.VMEM((ROW, 8, TOK), F32),
            pltpu.VMEM((ROW, 8, TOK), F32),
            pltpu.VMEM((TOK, 1024), F32),
            pltpu.VMEM((TOK, 1024), F32),
            pltpu.VMEM((8, TOK), F32),
            pltpu.VMEM((TP, 8, TOK), F32),
            pltpu.VMEM((ROW, 8, TOK), F32),
            pltpu.SemaphoreType.DMA((2, 2, 8)),
            pltpu.SemaphoreType.DMA((2, 2, 8)),
            pltpu.SemaphoreType.DMA((3,)),
            pltpu.SemaphoreType.DMA((3,)),
            pltpu.SemaphoreType.DMA((3, 4)),
            pltpu.SemaphoreType.DMA((3, 4)),
            pltpu.SemaphoreType.DMA((3,)),
            pltpu.SemaphoreType.DMA((3,)),
            pltpu.SemaphoreType.DMA((6,)),
            pltpu.SemaphoreType.DMA((6,)),
        ],
        compiler_params=pltpu.CompilerParams(
            collective_id=0, has_side_effects=True, vmem_limit_bytes=48 << 20
        ),
    )(
        queries, keys, values, mixer_input, gate, step_weight, state_weight, step_bias,
        decay_rate, skip_gain, norm_gain.reshape(1, -1),
    )


def solution(mesh):
    return jax.shard_map(
        per_device,
        mesh=mesh,
        in_specs=(P("ctx", "tp"),) * 5 + (P("tp", None),) * 2 + (P("tp"),) * 4,
        out_specs=(P("ctx", "tp"), P("ctx", "tp")),
        check_vma=False,
    )
```

```python
import functools
import math

import jax
import jax.numpy as jnp
from jax import lax
from jax.experimental import pallas as pl
from jax.experimental.pallas import tpu as pltpu
from jax.sharding import PartitionSpec as P

HD = 128
TOK = 128
ROW = 16
ROWS = 4
TP = 8
HEADS = 16
STATE = 16
PAIRS = 8
CHANNELS = 8192
SCALE2 = math.log2(math.e) / math.sqrt(HD)
F32 = jnp.float32
BF16 = jnp.bfloat16
EXACT = lax.Precision.HIGHEST
MESH = pl.DeviceIdType.MESH


def dot(a, b, precision=None):
    return jnp.dot(a, b, preferred_element_type=F32, precision=precision)


def dot_t(a, b, precision=None):
    return lax.dot_general(
        a, b, (((1,), (1,)), ((), ())), preferred_element_type=F32, precision=precision
    )


def kernel(
    q_hbm, k_hbm, v_hbm, x_hbm, gate_hbm, ws_hbm, wm_hbm, bias_hbm, rate_hbm, skip_hbm, norm_hbm,
    attn_ref, mamba_ref,
    q_ref, x_ref, gate_ref, ws_ref, wm_ref, bias_ref, rate_ref, skip_ref, norm_ref,
    kbuf, vbuf, qbuf, obuf, orecv, stat_send, stat_recv, own_out, acc_out, part, part_stat,
    proj_send, proj_recv, csend, crecv, fsend, frecv, ysend, yrecv, rsend, srecv,
    base, gated, sqsend, sqrecv, pref,
    load_sem, ring_ss, ring_rs, q_ss, q_rs, o_ss, o_rs, st_ss, st_rs, grp_ss, grp_rs, known,
):
    me = lax.axis_index("ctx")
    t = lax.axis_index("tp")
    y, z = me // ROW, me % ROW

    def tp_peer(o):
        return lax.rem(t + o, TP)

    def z_peer(o):
        return y * ROW + lax.rem(z + o + ROW, ROW)

    def y_peer(o):
        return lax.rem(y + o + ROWS, ROWS) * ROW + z

    def at(ctx, tp):
        return {"ctx": ctx, "tp": tp}

    def signal(sem, ctx, tp):
        pl.semaphore_signal(sem, inc=1, device_id=at(ctx, tp), device_id_type=MESH)

    barrier = pltpu.get_barrier_semaphore()
    for o in range(1, TP):
        signal(barrier, me, tp_peer(o))
    for o in (1, -1):
        signal(barrier, z_peer(o), t)
    for o in range(1, ROWS):
        signal(barrier, y_peer(o), t)

    loads = [
        pltpu.make_async_copy(src, dst, load_sem.at[i])
        for i, (src, dst) in enumerate((
            (x_hbm, x_ref), (ws_hbm, ws_ref), (wm_hbm, wm_ref), (bias_hbm, bias_ref),
            (rate_hbm, rate_ref), (skip_hbm, skip_ref), (k_hbm, kbuf.at[4]), (v_hbm, vbuf.at[4]),
            (q_hbm, q_ref), (gate_hbm, gate_ref), (norm_hbm, norm_ref),
        ))
    ]
    for copy in loads:
        copy.start()

    def remote(src, dst, ssem, rsem, ctx, tp):
        return pltpu.make_async_remote_copy(
            src_ref=src, dst_ref=dst, send_sem=ssem, recv_sem=rsem,
            device_id=at(ctx, tp), device_id_type=MESH,
        )

    pl.semaphore_wait(barrier, TP - 1 + 2 + ROWS - 1)

    def ring_copy(kv, d, s):
        buf = (kbuf, vbuf)[kv]
        i = 0 if d > 0 else 1
        src = (k_hbm, v_hbm)[kv] if s == 1 else buf.at[(4 - d * (s - 1)) % ROW]
        return remote(
            src, buf.at[(4 - d * s) % ROW], ring_ss.at[kv, i, s - 1], ring_rs.at[kv, i, s - 1],
            z_peer(d), t,
        )

    def ring_steps(d):
        return ROW // 2 if d > 0 else ROW // 2 - 1

    for kv in (0, 1):
        for d in (1, -1):
            ring_copy(kv, d, 1).start()
    for o in (1, -1):
        signal(known.at[0], z_peer(o), t)

    def ring(s):
        for kv in (0, 1):
            for d in (1, -1):
                if s <= ring_steps(d):
                    ring_copy(kv, d, s).wait_recv()
                    if s + 1 <= ring_steps(d):
                        ring_copy(kv, d, s + 1).start()

    def q_copy(o):
        return remote(q_hbm, qbuf.at[o - 1], q_ss.at[o - 1], q_rs.at[o - 1], y_peer(-o), t)

    for o in range(1, ROWS):
        @pl.when(y >= o)
        def _(o=o):
            q_copy(o).start()

    for copy in loads[:6]:
        copy.wait()
    step_part = dot(x_ref[...], ws_ref[...]).T
    maps_part = dot_t(wm_ref[...], x_ref[...])
    for p in range(TP):
        proj_send[p, 0:16, :] = step_part[16 * p:16 * p + 16]
        proj_send[p, 16:48, :] = maps_part

    def proj_copy(o):
        return remote(
            proj_send.at[tp_peer(o)], proj_recv.at[t], grp_ss.at[0], grp_rs.at[0], me, tp_peer(o)
        )

    for o in range(1, TP):
        proj_copy(o).start()

    lane = lax.broadcasted_iota(jnp.int32, (TOK, TOK), 1)
    sub = lax.broadcasted_iota(jnp.int32, (TOK, TOK), 0)
    low = lane < 64
    sub16 = lax.broadcasted_iota(jnp.int32, (HEADS, TOK), 0)
    lane16 = lax.broadcasted_iota(jnp.int32, (HEADS, TOK), 1)

    def column(ref):
        out = jnp.full((HEADS, TOK), ref[0], F32)
        for h in range(1, HEADS):
            out = jnp.where(sub16 == h, ref[h], out)
        return out

    bias, rate = column(bias_ref), column(rate_ref)
    pl.semaphore_wait(known.at[0], 2)
    for o in (2, -2):
        signal(known.at[1], z_peer(o), t)

    ring(1)
    pl.semaphore_wait(known.at[1], 2)
    for o in (4, -4):
        signal(known.at[2], z_peer(o), t)
    ring(2)

    remote(
        proj_send.at[0:TP - 1], proj_recv.at[0:TP - 1], grp_ss.at[0], grp_rs.at[0], me, tp_peer(1)
    ).wait_recv()
    proj_recv[t] = proj_send[t]
    total = proj_recv[0]
    for p in range(1, TP):
        total = total + proj_recv[p]
    b_rows, c_rows = total[16:32], total[32:48]
    raw = total[0:16] + bias
    step = jnp.maximum(raw, 0.0) + jnp.log1p(jnp.exp(-jnp.abs(raw)))
    climb = -rate * step
    for sh in (1, 2, 4, 8, 16, 32, 64):
        climb = climb + jnp.where(lane16 >= sh, pltpu.roll(climb, sh, axis=1), 0.0)
    final = jnp.broadcast_to(climb[:, TOK - 1:TOK], (HEADS, TOK))
    for j in range(PAIRS):
        fsend[j] = jnp.where(low[0:1], final[2 * j:2 * j + 1], final[2 * j + 1:2 * j + 2])
    feed_weight = jnp.exp(final - climb) * step

    def pair_input(j):
        xp = x_ref[:, 128 * j:128 * j + 128]
        zero = jnp.zeros_like(xp)
        return jnp.concatenate([jnp.where(low, xp, zero), jnp.where(low, zero, xp)], axis=0)

    for j in range(PAIRS):
        feed = jnp.concatenate(
            [b_rows * feed_weight[h:h + 1] for h in (2 * j, 2 * j + 1)], axis=1
        ).astype(BF16)
        contrib = dot(feed, pair_input(j))
        csend[2 * j] = contrib[0:8]
        csend[2 * j + 1] = contrib[8:16]

    pl.semaphore_wait(known.at[2], 2)

    def f_copy(o):
        return remote(
            fsend.at[lax.rem(z + o, ROW) // 2], frecv.at[z], grp_ss.at[1], grp_rs.at[1],
            z_peer(o), t,
        )

    def c_copy(o):
        return remote(
            csend.at[lax.rem(z + o, ROW)], crecv.at[z], grp_ss.at[2], grp_rs.at[2], z_peer(o), t
        )

    for o in (8, 7, 9, 6, 10, 5, 11, 4, 12, 3, 13, 2, 14, 1, 15):
        f_copy(o).start()
        c_copy(o).start()
    crecv[z] = csend[z]
    frecv[z] = fsend[z // 2]
    ring(3)
    turned = jnp.concatenate([c_rows, climb, jnp.exp(climb), jnp.zeros((80, TOK), F32)], axis=0).T
    c_cols = turned[:, 0:16]
    inner = dot(c_cols, b_rows, EXACT)
    causal = sub >= lane

    def local_pair(j):
        mixes = []
        for h in (2 * j, 2 * j + 1):
            diff = turned[:, 16 + h:17 + h] - climb[h:h + 1]
            mix = inner * jnp.exp(diff) * step[h:h + 1]
            mixes.append(jnp.where(causal, mix, 0.0).astype(BF16))
        out = dot(jnp.concatenate(mixes, axis=1), pair_input(j))
        gain = jnp.where(low, skip_ref[2 * j], skip_ref[2 * j + 1])
        cols = slice(128 * j, 128 * j + 128)
        base[:, cols] = out + gain * x_ref[:, cols].astype(F32)

    for j in range(PAIRS):
        local_pair(j)

    half_keys = 8 * TOK
    slot = lax.broadcasted_iota(jnp.int32, (1, half_keys), 1)
    query_row = lax.broadcasted_iota(jnp.int32, (2 * TOK, 1), 0)
    query_row = jnp.where(query_row >= TOK, query_row - TOK, query_row) + z * TOK
    lane2 = lax.broadcasted_iota(jnp.int32, (2 * TOK, TOK), 1)

    def scores_of(o, pair, side):
        src = q_ref if o == 0 else qbuf.at[o - 1]
        q = jnp.concatenate(
            [src[:, 128 * h:128 * h + 128] for h in (2 * pair, 2 * pair + 1)], axis=0
        )
        out = dot_t(q, kbuf[8 * side:8 * side + 8].reshape(half_keys, HD))
        if o == 0:
            block = lax.rem(slot // TOK + (z + 8 * side - 4 + ROW), ROW)
            out = jnp.where(block * TOK + slot % TOK <= query_row, out, -1e30)
        return out

    def first_half(o, pair):
        scores = scores_of(o, pair, 0)
        top = jnp.max(scores, axis=1, keepdims=True)
        weights = jnp.exp2((scores - top) * SCALE2)
        whole = jnp.sum(weights, axis=1, keepdims=True)
        part[o, pair] = dot(weights.astype(BF16), vbuf[0:8].reshape(half_keys, HD))
        part_stat[o, pair] = jnp.where(lane2 == 0, top, whole)

    def second_half(o, pair):
        scores = scores_of(o, pair, 1)
        stat = part_stat[o, pair]
        before = stat[:, 0:1]
        top = jnp.maximum(before, jnp.max(scores, axis=1, keepdims=True))
        weights = jnp.exp2((scores - top) * SCALE2)
        keep = jnp.exp2((before - top) * SCALE2)
        whole = stat[:, 1:2] * keep + jnp.sum(weights, axis=1, keepdims=True)
        mixed = part[o, pair] * keep + dot(
            weights.astype(BF16), vbuf[8:16].reshape(half_keys, HD)
        )
        return mixed / whole, top, whole

    def first_halves(o):
        @pl.when(y + o < ROWS)
        def _():
            if o:
                q_copy(o).wait_recv()
            for pair in (0, 1):
                first_half(o, pair)

    for copy in loads[6:]:
        copy.wait()
    ring(4)
    first_halves(1)
    ring(5)

    first_halves(2)
    ring(6)
    remote(
        frecv.at[0:ROW - 1], frecv.at[0:ROW - 1], grp_ss.at[1], grp_rs.at[1], z_peer(1), t
    ).wait_recv()
    remote(
        csend.at[0:ROW - 1], crecv.at[0:ROW - 1], grp_ss.at[2], grp_rs.at[2], z_peer(1), t
    ).wait_recv()
    running = jnp.zeros((8, TOK), F32)
    passed = jnp.zeros((1, TOK), F32)
    gone = []
    for b in range(ROW):
        pref[b] = running
        gone.append(passed)
        running = jnp.exp(frecv[b]) * running + crecv[b]
        passed = passed + frecv[b]
    ysend[0:8] = running
    ysend[8:16] = jnp.broadcast_to(passed, (8, TOK))

    def y_copy(o):
        return remote(ysend, yrecv.at[y], grp_ss.at[3], grp_rs.at[3], y_peer(o), t)

    for o in (2, 1, 3):
        y_copy(o).start()
    yrecv[y] = ysend[...]
    first_halves(3)
    ring(7)
    remote(
        yrecv.at[0:ROWS - 1], yrecv.at[0:ROWS - 1], grp_ss.at[3], grp_rs.at[3], y_peer(1), t
    ).wait_recv()
    enter = jnp.zeros((8, TOK), F32)
    for r in range(ROWS - 1):
        longer = jnp.exp(yrecv[r, 8:16]) * enter + yrecv[r, 0:8]
        enter = jnp.where(r < y, longer, enter)
    for b in range(ROW):
        rsend[b] = pref[b] + jnp.exp(gone[b]) * enter

    def r_copy(o):
        return remote(
            rsend.at[lax.rem(z + o, ROW)], srecv.at[z], grp_ss.at[4], grp_rs.at[4], z_peer(o), t
        )

    for o in (8, 7, 9, 6, 10, 5, 11, 4, 12, 3, 13, 2, 14, 1, 15):
        r_copy(o).start()
    srecv[z] = rsend[z]
    first_halves(0)
    ring(8)

    def stats_of(tops, wholes):
        out = jnp.zeros((TOK, TOK), F32)
        for i, col in enumerate(tops + wholes):
            out = jnp.where(lane == i, col, out)
        return out

    def o_copy(o, pair):
        return remote(
            obuf.at[o - 1, pair], orecv.at[o - 1, pair],
            o_ss.at[o - 1, pair], o_rs.at[o - 1, pair], y_peer(o), t,
        )

    def st_copy(o):
        return remote(
            stat_send.at[o - 1], stat_recv.at[o - 1], st_ss.at[o - 1], st_rs.at[o - 1],
            y_peer(o), t,
        )

    for o in (3, 2, 1):
        @pl.when(y + o < ROWS)
        def _(o=o):
            tops, wholes = [], []
            for pair in (0, 1):
                mixed, top, whole = second_half(o, pair)
                obuf[o - 1, pair] = mixed.astype(BF16)
                o_copy(o, pair).start()
                tops += [top[0:TOK], top[TOK:]]
                wholes += [whole[0:TOK], whole[TOK:]]
            stat_send[o - 1] = stats_of(tops, wholes).T[0:8]
            st_copy(o).start()

    tops, wholes = [], []
    for pair in (0, 1):
        mixed, top, whole = second_half(0, pair)
        acc_out[:, 256 * pair:256 * pair + 128] = mixed[0:TOK]
        acc_out[:, 256 * pair + 128:256 * pair + 256] = mixed[TOK:]
        tops += [top[0:TOK], top[TOK:]]
        wholes += [whole[0:TOK], whole[TOK:]]
    own_out[...] = stats_of(tops, wholes)

    remote(
        rsend.at[0:ROW - 1], srecv.at[0:ROW - 1], grp_ss.at[4], grp_rs.at[4], z_peer(1), t
    ).wait_recv()
    squares = jnp.zeros((TOK, TOK), F32)
    for j in range(PAIRS):
        cols = slice(128 * j, 128 * j + 128)
        state = srecv[2 * j:2 * j + 2].reshape(STATE, TOK)
        grown = jnp.where(low, turned[:, 32 + 2 * j:33 + 2 * j], turned[:, 33 + 2 * j:34 + 2 * j])
        out = base[:, cols] + grown * dot(c_cols, state, EXACT)
        g = gate_ref[:, cols].astype(F32)
        out = out * (g / (1.0 + jnp.exp(-g)))
        gated[:, cols] = out
        squares = squares + out * out
    sqsend[...] = dot_t(jnp.ones((8, TOK), F32), squares, EXACT)

    def sq_copy(o):
        return remote(sqsend, sqrecv.at[t], grp_ss.at[5], grp_rs.at[5], me, tp_peer(o))

    for o in range(1, TP):
        sq_copy(o).start()
    sqrecv[t] = sqsend[...]

    for o in range(1, ROWS):
        @pl.when(y >= o)
        def _(o=o):
            st_copy(o).wait_recv()
            other = jnp.concatenate([stat_recv[o - 1], jnp.zeros((120, TOK), F32)], axis=0).T
            mine = own_out[...]
            tops, wholes = [], []
            for h in range(4):
                if h % 2 == 0:
                    o_copy(o, h // 2).wait_recv()
                cols = slice(128 * h, 128 * h + 128)
                rows = slice(128 * (h % 2), 128 * (h % 2) + 128)
                top_a, top_b = mine[:, h:h + 1], other[:, h:h + 1]
                top = jnp.maximum(top_a, top_b)
                part_a = mine[:, 4 + h:5 + h] * jnp.exp2((top_a - top) * SCALE2)
                part_b = other[:, 4 + h:5 + h] * jnp.exp2((top_b - top) * SCALE2)
                whole = part_a + part_b
                acc_out[:, cols] = (
                    acc_out[:, cols] * (part_a / whole)
                    + orecv[o - 1, h // 2, rows].astype(F32) * (part_b / whole)
                )
                tops.append(top)
                wholes.append(whole)
            own_out[...] = stats_of(tops, wholes)

    attn_ref[...] = acc_out[...].astype(BF16)

    remote(
        sqrecv.at[0:TP - 1], sqrecv.at[0:TP - 1], grp_ss.at[5], grp_rs.at[5], me, tp_peer(1)
    ).wait_recv()
    square = sqrecv[0]
    for p in range(1, TP):
        square = square + sqrecv[p]
    inverse = lax.rsqrt(square[0:1] / CHANNELS + 1e-5)
    inverse = jnp.broadcast_to(inverse, (TOK, TOK)).T
    for j in range(PAIRS):
        cols = slice(128 * j, 128 * j + 128)
        mamba_ref[:, cols] = (gated[:, cols] * inverse * norm_ref[0:1, cols]).astype(BF16)

    remote(
        proj_send.at[0:TP - 1], proj_recv.at[0:TP - 1], grp_ss.at[0], grp_rs.at[0], me, tp_peer(1)
    ).wait_send()
    remote(
        frecv.at[0:ROW - 1], frecv.at[0:ROW - 1], grp_ss.at[1], grp_rs.at[1], z_peer(1), t
    ).wait_send()
    remote(
        csend.at[0:ROW - 1], crecv.at[0:ROW - 1], grp_ss.at[2], grp_rs.at[2], z_peer(1), t
    ).wait_send()
    remote(
        yrecv.at[0:ROWS - 1], yrecv.at[0:ROWS - 1], grp_ss.at[3], grp_rs.at[3], y_peer(1), t
    ).wait_send()
    remote(
        rsend.at[0:ROW - 1], srecv.at[0:ROW - 1], grp_ss.at[4], grp_rs.at[4], z_peer(1), t
    ).wait_send()
    remote(
        sqrecv.at[0:TP - 1], sqrecv.at[0:TP - 1], grp_ss.at[5], grp_rs.at[5], me, tp_peer(1)
    ).wait_send()
    for kv in (0, 1):
        for d in (1, -1):
            for s in range(1, ring_steps(d) + 1):
                ring_copy(kv, d, s).wait_send()
    for o in range(1, ROWS):
        @pl.when(y >= o)
        def _(o=o):
            q_copy(o).wait_send()

        @pl.when(y + o < ROWS)
        def _(o=o):
            for pair in (0, 1):
                o_copy(o, pair).wait_send()
            st_copy(o).wait_send()


def per_device(
    queries, keys, values, mixer_input, gate, step_weight, state_weight, step_bias, decay_rate,
    skip_gain, norm_gain,
):
    vmem = pl.BlockSpec(memory_space=pltpu.VMEM)
    hbm = pl.BlockSpec(memory_space=pltpu.HBM)
    return pl.pallas_call(
        kernel,
        out_shape=(
            jax.ShapeDtypeStruct((TOK, 4 * HD), BF16),
            jax.ShapeDtypeStruct((TOK, 1024), BF16),
        ),
        in_specs=[hbm] * 11,
        out_specs=(vmem, vmem),
        scratch_shapes=[
            pltpu.VMEM((TOK, 4 * HD), BF16),
            pltpu.VMEM((TOK, 1024), BF16),
            pltpu.VMEM((TOK, 1024), BF16),
            pltpu.VMEM((1024, 128), BF16),
            pltpu.VMEM((32, 1024), BF16),
            pltpu.SMEM((HEADS,), F32),
            pltpu.SMEM((HEADS,), F32),
            pltpu.SMEM((HEADS,), F32),
            pltpu.VMEM((1, 1024), F32),
            pltpu.VMEM((ROW, TOK, HD), BF16),
            pltpu.VMEM((ROW, TOK, HD), BF16),
            pltpu.VMEM((3, TOK, 4 * HD), BF16),
            pltpu.VMEM((3, 2, 2 * TOK, HD), BF16),
            pltpu.VMEM((3, 2, 2 * TOK, HD), BF16),
            pltpu.VMEM((3, 8, TOK), F32),
            pltpu.VMEM((3, 8, TOK), F32),
            pltpu.VMEM((TOK, TOK), F32),
            pltpu.VMEM((TOK, 4 * HD), F32),
            pltpu.VMEM((4, 2, 2 * TOK, HD), F32),
            pltpu.VMEM((4, 2, 2 * TOK, TOK), F32),
            pltpu.VMEM((TP, 48, TOK), F32),
            pltpu.VMEM((TP, 48, TOK), F32),
            pltpu.VMEM((ROW, 8, TOK), F32),
            pltpu.VMEM((ROW, 8, TOK), F32),
            pltpu.VMEM((PAIRS, 1, TOK), F32),
            pltpu.VMEM((ROW, 1, TOK), F32),
            pltpu.VMEM((16, TOK), F32),
            pltpu.VMEM((ROWS, 16, TOK), F32),
            pltpu.VMEM((ROW, 8, TOK), F32),
            pltpu.VMEM((ROW, 8, TOK), F32),
            pltpu.VMEM((TOK, 1024), F32),
            pltpu.VMEM((TOK, 1024), F32),
            pltpu.VMEM((8, TOK), F32),
            pltpu.VMEM((TP, 8, TOK), F32),
            pltpu.VMEM((ROW, 8, TOK), F32),
            pltpu.SemaphoreType.DMA((11,)),
            pltpu.SemaphoreType.DMA((2, 2, 8)),
            pltpu.SemaphoreType.DMA((2, 2, 8)),
            pltpu.SemaphoreType.DMA((3,)),
            pltpu.SemaphoreType.DMA((3,)),
            pltpu.SemaphoreType.DMA((3, 2)),
            pltpu.SemaphoreType.DMA((3, 2)),
            pltpu.SemaphoreType.DMA((3,)),
            pltpu.SemaphoreType.DMA((3,)),
            pltpu.SemaphoreType.DMA((6,)),
            pltpu.SemaphoreType.DMA((6,)),
            pltpu.SemaphoreType.REGULAR((3,)),
        ],
        compiler_params=pltpu.CompilerParams(
            collective_id=0, has_side_effects=True, vmem_limit_bytes=48 << 20
        ),
    )(*[pltpu.with_memory_space_constraint(a, pltpu.HBM) for a in (
        queries, keys, values, mixer_input, gate, step_weight, state_weight.T, step_bias,
        decay_rate, skip_gain, norm_gain.reshape(1, -1),
    )])


def solution(mesh):
    return jax.shard_map(
        per_device,
        mesh=mesh,
        in_specs=(P("ctx", "tp"),) * 5 + (P("tp", None),) * 2 + (P("tp"),) * 4,
        out_specs=(P("ctx", "tp"), P("ctx", "tp")),
        check_vma=False,
    )
```

```python
import functools
import math

import jax
import jax.numpy as jnp
from jax import lax
from jax.experimental import pallas as pl
from jax.experimental.pallas import tpu as pltpu
from jax.sharding import PartitionSpec as P

HD = 128
TOK = 128
ROW = 16
ROWS = 4
TP = 8
HEADS = 16
STATE = 16
PAIRS = 8
CHANNELS = 8192
SCALE2 = math.log2(math.e) / math.sqrt(HD)
F32 = jnp.float32
BF16 = jnp.bfloat16
EXACT = lax.Precision.HIGHEST
MESH = pl.DeviceIdType.MESH


SLOTS = (-2, -1, 0, 1, 2, 3, 4, -3, -4, 5, 6, -5, -6, 7, -7, -8)
PARTS = ((0, 5), (5, 9), (9, 13), (13, 16))


def slot_of(r):
    return SLOTS.index(r)


def dot(a, b, precision=None):
    return jnp.dot(a, b, preferred_element_type=F32, precision=precision)


def dot_t(a, b, precision=None):
    return lax.dot_general(
        a, b, (((1,), (1,)), ((), ())), preferred_element_type=F32, precision=precision
    )


def kernel(
    q_hbm, k_hbm, v_hbm, x_hbm, gate_hbm, ws_hbm, wm_hbm, bias_hbm, rate_hbm, skip_hbm, norm_hbm,
    attn_ref, mamba_ref,
    q_ref, x_ref, gate_ref, ws_ref, wm_ref, bias_ref, rate_ref, skip_ref, norm_ref,
    kbuf, vbuf, qbuf, obuf, orecv, stat_send, stat_recv, part, part_stat,
    proj_send, proj_recv, csend, crecv, fsend, frecv, ysend, yrecv, rsend, srecv,
    base, gated, sqsend, sqrecv, pref,
    load_sem, ring_ss, ring_rs, q_ss, q_rs, o_ss, o_rs, st_ss, st_rs, y_ss, y_rs, grp_ss, grp_rs, known,
):
    me = lax.axis_index("ctx")
    t = lax.axis_index("tp")
    y, z = me // ROW, me % ROW

    def tp_peer(o):
        return lax.rem(t + o, TP)

    def z_peer(o):
        return y * ROW + lax.rem(z + o + ROW, ROW)

    def y_peer(o):
        return lax.rem(y + o + ROWS, ROWS) * ROW + z

    def at(ctx, tp):
        return {"ctx": ctx, "tp": tp}

    def signal(sem, ctx, tp):
        pl.semaphore_signal(sem, inc=1, device_id=at(ctx, tp), device_id_type=MESH)

    barrier = pltpu.get_barrier_semaphore()
    for o in range(1, TP):
        signal(barrier, me, tp_peer(o))
    for o in (1, -1):
        signal(barrier, z_peer(o), t)
    for o in range(1, ROWS):
        signal(barrier, y_peer(o), t)

    loads = [
        pltpu.make_async_copy(src, dst, load_sem.at[i])
        for i, (src, dst) in enumerate((
            (x_hbm, x_ref), (ws_hbm, ws_ref), (wm_hbm, wm_ref), (bias_hbm, bias_ref),
            (rate_hbm, rate_ref), (skip_hbm, skip_ref), (k_hbm, kbuf.at[slot_of(0)]), (v_hbm, vbuf.at[slot_of(0)]),
            (q_hbm, q_ref), (gate_hbm, gate_ref), (norm_hbm, norm_ref),
        ))
    ]
    for copy in loads:
        copy.start()

    def remote(src, dst, ssem, rsem, ctx, tp):
        return pltpu.make_async_remote_copy(
            src_ref=src, dst_ref=dst, send_sem=ssem, recv_sem=rsem,
            device_id=at(ctx, tp), device_id_type=MESH,
        )

    pl.semaphore_wait(barrier, TP - 1 + 2 + ROWS - 1)

    def ring_copy(kv, d, s):
        buf = (kbuf, vbuf)[kv]
        i = 0 if d > 0 else 1
        src = (k_hbm, v_hbm)[kv] if s == 1 else buf.at[slot_of(-d * (s - 1))]
        return remote(
            src, buf.at[slot_of(-d * s)], ring_ss.at[kv], ring_rs.at[kv, i, s - 1], z_peer(d), t
        )

    def ring_steps(d):
        return ROW // 2 if d > 0 else ROW // 2 - 1

    pieces = [(kv, d) for kv in (0, 1) for d in (1, -1)]
    for kv, d in pieces:
        ring_copy(kv, d, 1).start()
    for o in (1, -1):
        signal(known.at[0], z_peer(o), t)

    def ring(s):
        for kv, d in pieces:
            if s <= ring_steps(d):
                ring_copy(kv, d, s).wait_recv()
                if s + 1 <= ring_steps(d):
                    ring_copy(kv, d, s + 1).start()

    def q_copy(o):
        return remote(q_hbm, qbuf.at[o - 1], q_ss.at[o - 1], q_rs.at[o - 1], y_peer(-o), t)

    for o in range(1, ROWS):
        @pl.when(y >= o)
        def _(o=o):
            q_copy(o).start()

    for copy in loads[:6]:
        copy.wait()
    step_part = dot(x_ref[...], ws_ref[...]).T
    maps_part = dot_t(wm_ref[...], x_ref[...])
    for p in range(TP):
        proj_send[p, 0:16, :] = step_part[16 * p:16 * p + 16]
        proj_send[p, 16:48, :] = maps_part

    def proj_copy(o):
        return remote(
            proj_send.at[tp_peer(o)], proj_recv.at[t], grp_ss.at[0], grp_rs.at[0], me, tp_peer(o)
        )

    for o in range(1, TP):
        proj_copy(o).start()

    lane = lax.broadcasted_iota(jnp.int32, (TOK, TOK), 1)
    sub = lax.broadcasted_iota(jnp.int32, (TOK, TOK), 0)
    low = lane < 64
    sub16 = lax.broadcasted_iota(jnp.int32, (HEADS, TOK), 0)
    lane16 = lax.broadcasted_iota(jnp.int32, (HEADS, TOK), 1)

    def column(ref):
        out = jnp.full((HEADS, TOK), ref[0], F32)
        for h in range(1, HEADS):
            out = jnp.where(sub16 == h, ref[h], out)
        return out

    bias, rate = column(bias_ref), column(rate_ref)
    pl.semaphore_wait(known.at[0], 2)
    for o in (2, -2):
        signal(known.at[1], z_peer(o), t)


    def greet_far():
        pl.semaphore_wait(known.at[1], 2)
        for o in (4, -4):
            signal(known.at[2], z_peer(o), t)

    pl.when(z >= 6)(greet_far)
    ring(1)
    ring(2)

    remote(
        proj_send.at[0:TP - 1], proj_recv.at[0:TP - 1], grp_ss.at[0], grp_rs.at[0], me, tp_peer(1)
    ).wait_recv()
    proj_recv[t] = proj_send[t]
    total = proj_recv[0]
    for p in range(1, TP):
        total = total + proj_recv[p]
    b_rows, c_rows = total[16:32], total[32:48]
    raw = total[0:16] + bias
    step = jnp.maximum(raw, 0.0) + jnp.log1p(jnp.exp(-jnp.abs(raw)))
    climb = -rate * step
    for sh in (1, 2, 4, 8, 16, 32, 64):
        climb = climb + jnp.where(lane16 >= sh, pltpu.roll(climb, sh, axis=1), 0.0)
    final = jnp.broadcast_to(climb[:, TOK - 1:TOK], (HEADS, TOK))
    for j in range(PAIRS):
        fsend[j] = jnp.where(low[0:1], final[2 * j:2 * j + 1], final[2 * j + 1:2 * j + 2])
    feed_weight = jnp.exp(final - climb) * step

    def pair_input(j):
        xp = x_ref[:, 128 * j:128 * j + 128]
        zero = jnp.zeros_like(xp)
        return jnp.concatenate([jnp.where(low, xp, zero), jnp.where(low, zero, xp)], axis=0)

    for j in range(PAIRS):
        feed = jnp.concatenate(
            [b_rows * feed_weight[h:h + 1] for h in (2 * j, 2 * j + 1)], axis=1
        ).astype(BF16)
        csend[j] = dot(feed, pair_input(j)).astype(BF16)

    pl.when(z < 6)(greet_far)
    pl.semaphore_wait(known.at[2], 2)

    def f_copy(o):
        return remote(
            fsend.at[lax.rem(z + o, PAIRS)], frecv.at[z], grp_ss.at[1], grp_rs.at[1],
            z_peer(o), t,
        )

    def c_copy(o):
        return remote(
            csend.at[lax.rem(z + o, PAIRS)], crecv.at[z], grp_ss.at[2], grp_rs.at[2], z_peer(o), t
        )

    for o in (8, 7, 9, 6, 10, 5, 11, 4, 12, 3, 13, 2, 14, 1, 15):
        f_copy(o).start()
        c_copy(o).start()
    crecv[z] = csend[lax.rem(z, PAIRS)]
    frecv[z] = fsend[lax.rem(z, PAIRS)]
    ring(3)
    turned = jnp.concatenate([c_rows, climb, jnp.exp(climb), jnp.zeros((80, TOK), F32)], axis=0).T
    c_cols = turned[:, 0:16]
    inner = dot(c_cols, b_rows, EXACT)
    causal = sub >= lane

    def local_pair(j):
        mixes = []
        for h in (2 * j, 2 * j + 1):
            diff = turned[:, 16 + h:17 + h] - climb[h:h + 1]
            mix = inner * jnp.exp(diff) * step[h:h + 1]
            mixes.append(jnp.where(causal, mix, 0.0).astype(BF16))
        out = dot(jnp.concatenate(mixes, axis=1), pair_input(j))
        gain = jnp.where(low, skip_ref[2 * j], skip_ref[2 * j + 1])
        cols = slice(128 * j, 128 * j + 128)
        base[:, cols] = out + gain * x_ref[:, cols].astype(F32)

    for j in range(PAIRS):
        local_pair(j)

    query_row = lax.broadcasted_iota(jnp.int32, (4 * TOK, 1), 0) % TOK + z * TOK

    def attend(o, number):
        first, last = PARTS[number]
        src = q_ref if o == 0 else qbuf.at[o - 1]
        q = jnp.concatenate([src[:, 128 * h:128 * h + 128] for h in range(4)], axis=0)
        width = (last - first) * TOK
        scores = dot_t(q, kbuf[first:last].reshape(width, HD))
        blocks = [scores[:, TOK * i:TOK * i + TOK] for i in range(last - first)]
        if o == 0:
            place = lax.broadcasted_iota(jnp.int32, (1, TOK), 1)
            blocks = [
                jnp.where(
                    place + lax.rem(z + SLOTS[first + i] + ROW, ROW) * TOK <= query_row, b, -1e30
                )
                for i, b in enumerate(blocks)
            ]
        top = blocks[0]
        for b in blocks[1:]:
            top = jnp.maximum(top, b)
        top = jnp.broadcast_to(jnp.max(top, axis=1, keepdims=True), (4 * TOK, TOK))
        if number:
            before = part_stat[o]
            top = jnp.maximum(before, top)
        weights = jnp.concatenate(
            [jnp.exp2((b - top) * SCALE2).astype(BF16) for b in blocks], axis=1
        )
        held = vbuf[first:last].reshape(width, HD)
        mixed = dot(weights, jnp.concatenate([held, jnp.ones_like(held)], axis=1))
        if number:
            keep = jnp.exp2((before - top) * SCALE2)
            mixed = mixed + part[o] * jnp.concatenate([keep, keep], axis=1)
        if number == 3 and o:
            whole = mixed[:, HD:]
            obuf[o - 1] = (mixed[:, 0:HD] / whole).astype(BF16)
            stats = jnp.zeros((TOK, TOK), F32)
            for h in range(4):
                rows = slice(TOK * h, TOK * h + TOK)
                stats = jnp.where(lane == h, top[rows], stats)
                stats = jnp.where(lane == 4 + h, whole[rows], stats)
            stat_send[o - 1] = stats.T[0:8]
            return
        part[o] = mixed
        part_stat[o] = top

    def attend_some(number, *queries):
        for row in range(ROWS):
            mine = [o for o in queries if row + o < ROWS]
            if mine:
                @pl.when(y == row)
                def _(mine=mine):
                    if not number:
                        for o in mine:
                            if o:
                                q_copy(o).wait_recv()
                    for o in mine:
                        attend(o, number)

    for copy in loads[6:]:
        copy.wait()
    attend_some(0, 1, 2, 3, 0)
    ring(4)
    attend_some(1, 1, 2)
    remote(
        frecv.at[0:ROW - 1], frecv.at[0:ROW - 1], grp_ss.at[1], grp_rs.at[1], z_peer(1), t
    ).wait_recv()
    remote(
        crecv.at[0:ROW - 1], crecv.at[0:ROW - 1], grp_ss.at[2], grp_rs.at[2], z_peer(1), t
    ).wait_recv()
    running = jnp.zeros((STATE, TOK), F32)
    passed = jnp.zeros((1, TOK), F32)
    gone = []
    for b in range(ROW):
        pref[b] = running
        gone.append(passed)
        running = jnp.exp(frecv[b]) * running + crecv[b].astype(F32)
        passed = passed + frecv[b]
    ysend[0:16] = running
    ysend[16:24] = jnp.broadcast_to(passed, (8, TOK))

    def y_copy(o):
        return remote(ysend, yrecv.at[o - 1], y_ss.at[o - 1], y_rs.at[o - 1], y_peer(o), t)

    for o in range(1, ROWS):
        @pl.when(y + o < ROWS)
        def _(o=o):
            y_copy(o).start()

    ring(5)

    attend_some(1, 3, 0)
    for o in range(1, ROWS):
        @pl.when(y >= o)
        def _(o=o):
            y_copy(o).wait_recv()

        @pl.when(y < o)
        def _(o=o):
            yrecv[o - 1] = jnp.zeros((24, TOK), F32)

    enter = jnp.zeros((STATE, TOK), F32)
    for o in (3, 2, 1):
        enter = jnp.exp(yrecv[o - 1, 16:17]) * enter + yrecv[o - 1, 0:16]
    for b in range(ROW):
        rsend[b] = pref[b] + jnp.exp(gone[b]) * enter

    def r_copy(o):
        return remote(
            rsend.at[lax.rem(z + o + ROW, ROW)], srecv.at[lax.rem(z, PAIRS)],
            grp_ss.at[4], grp_rs.at[4], z_peer(o), t,
        )

    for o in (-4, 3, -3, 2, -2, 1, -1):
        r_copy(o).start()
    srecv[lax.rem(z, PAIRS)] = rsend[z]
    ring(6)
    attend_some(2, 3, 2)
    ring(7)
    attend_some(2, 1, 0)
    ring(8)

    def o_copy(o):
        return remote(
            obuf.at[o - 1], orecv.at[o - 1], o_ss.at[o - 1], o_rs.at[o - 1], y_peer(o), t
        )

    def st_copy(o):
        return remote(
            stat_send.at[o - 1], stat_recv.at[o - 1], st_ss.at[o - 1], st_rs.at[o - 1],
            y_peer(o), t,
        )

    attend_some(3, 3, 2, 1)
    for o in (3, 2, 1):
        @pl.when(y + o < ROWS)
        def _(o=o):
            o_copy(o).start()
            st_copy(o).start()

    remote(
        srecv.at[0:PAIRS - 1], srecv.at[0:PAIRS - 1], grp_ss.at[4], grp_rs.at[4], z_peer(1), t
    ).wait_recv()
    squares = jnp.zeros((TOK, TOK), F32)
    for j in range(PAIRS):
        cols = slice(128 * j, 128 * j + 128)
        state = srecv[j]
        grown = jnp.where(low, turned[:, 32 + 2 * j:33 + 2 * j], turned[:, 33 + 2 * j:34 + 2 * j])
        out = base[:, cols] + grown * dot(c_cols, state, EXACT)
        g = gate_ref[:, cols].astype(F32)
        out = out * (g / (1.0 + jnp.exp(-g)))
        gated[:, cols] = out
        squares = squares + out * out
    sqsend[...] = dot_t(jnp.ones((8, TOK), F32), squares, EXACT)

    def sq_copy(o):
        return remote(sqsend, sqrecv.at[t], grp_ss.at[5], grp_rs.at[5], me, tp_peer(o))

    for o in range(1, TP):
        sq_copy(o).start()
    sqrecv[t] = sqsend[...]

    attend(0, 3)
    for o in range(1, ROWS):
        @pl.when(y >= o)
        def _(o=o):
            st_copy(o).wait_recv()
            o_copy(o).wait_recv()
            other = jnp.concatenate([stat_recv[o - 1], jnp.zeros((120, TOK), F32)], axis=0).T
            for h in range(4):
                rows = slice(TOK * h, TOK * h + TOK)
                before, theirs = part_stat[0, rows], other[:, h:h + 1]
                top = jnp.maximum(before, theirs)
                keep = jnp.exp2((before - top) * SCALE2)
                gain = other[:, 4 + h:5 + h] * jnp.exp2((theirs - top) * SCALE2)
                part[0, rows, 0:HD] = (
                    part[0, rows, 0:HD] * keep + orecv[o - 1, rows].astype(F32) * gain
                )
                part[0, rows, HD:] = part[0, rows, HD:] * keep + gain
                part_stat[0, rows] = top

    for h in range(4):
        rows = slice(TOK * h, TOK * h + TOK)
        attn_ref[:, rows] = (part[0, rows, 0:HD] / part[0, rows, HD:]).astype(BF16)

    remote(
        sqrecv.at[0:TP - 1], sqrecv.at[0:TP - 1], grp_ss.at[5], grp_rs.at[5], me, tp_peer(1)
    ).wait_recv()
    square = sqrecv[0]
    for p in range(1, TP):
        square = square + sqrecv[p]
    inverse = lax.rsqrt(square[0:1] / CHANNELS + 1e-5)
    inverse = jnp.broadcast_to(inverse, (TOK, TOK)).T
    for j in range(PAIRS):
        cols = slice(128 * j, 128 * j + 128)
        mamba_ref[:, cols] = (gated[:, cols] * inverse * norm_ref[0:1, cols]).astype(BF16)

    remote(
        proj_send.at[0:TP - 1], proj_recv.at[0:TP - 1], grp_ss.at[0], grp_rs.at[0], me, tp_peer(1)
    ).wait_send()
    remote(
        frecv.at[0:ROW - 1], frecv.at[0:ROW - 1], grp_ss.at[1], grp_rs.at[1], z_peer(1), t
    ).wait_send()
    remote(
        crecv.at[0:ROW - 1], crecv.at[0:ROW - 1], grp_ss.at[2], grp_rs.at[2], z_peer(1), t
    ).wait_send()
    remote(
        srecv.at[0:PAIRS - 1], srecv.at[0:PAIRS - 1], grp_ss.at[4], grp_rs.at[4], z_peer(1), t
    ).wait_send()
    remote(
        sqrecv.at[0:TP - 1], sqrecv.at[0:TP - 1], grp_ss.at[5], grp_rs.at[5], me, tp_peer(1)
    ).wait_send()
    for kv, buf in ((0, kbuf), (1, vbuf)):
        remote(
            buf.at[0:ROW - 1], buf.at[0:ROW - 1], ring_ss.at[kv], ring_rs.at[kv, 0, 0], z_peer(1), t
        ).wait_send()
    for o in range(1, ROWS):
        @pl.when(y >= o)
        def _(o=o):
            q_copy(o).wait_send()

        @pl.when(y + o < ROWS)
        def _(o=o):
            o_copy(o).wait_send()
            y_copy(o).wait_send()
            st_copy(o).wait_send()


def per_device(
    queries, keys, values, mixer_input, gate, step_weight, state_weight, step_bias, decay_rate,
    skip_gain, norm_gain,
):
    vmem = pl.BlockSpec(memory_space=pltpu.VMEM)
    hbm = pl.BlockSpec(memory_space=pltpu.HBM)
    return pl.pallas_call(
        kernel,
        out_shape=(
            jax.ShapeDtypeStruct((TOK, 4 * HD), BF16),
            jax.ShapeDtypeStruct((TOK, 1024), BF16),
        ),
        in_specs=[hbm] * 11,
        out_specs=(vmem, vmem),
        scratch_shapes=[
            pltpu.VMEM((TOK, 4 * HD), BF16),
            pltpu.VMEM((TOK, 1024), BF16),
            pltpu.VMEM((TOK, 1024), BF16),
            pltpu.VMEM((1024, 128), BF16),
            pltpu.VMEM((32, 1024), BF16),
            pltpu.SMEM((HEADS,), F32),
            pltpu.SMEM((HEADS,), F32),
            pltpu.SMEM((HEADS,), F32),
            pltpu.VMEM((1, 1024), F32),
            pltpu.VMEM((ROW, TOK, HD), BF16),
            pltpu.VMEM((ROW, TOK, HD), BF16),
            pltpu.VMEM((3, TOK, 4 * HD), BF16),
            pltpu.VMEM((3, 4 * TOK, HD), BF16),
            pltpu.VMEM((3, 4 * TOK, HD), BF16),
            pltpu.VMEM((3, 8, TOK), F32),
            pltpu.VMEM((3, 8, TOK), F32),
            pltpu.VMEM((4, 4 * TOK, 2 * HD), F32),
            pltpu.VMEM((4, 4 * TOK, TOK), F32),
            pltpu.VMEM((TP, 48, TOK), F32),
            pltpu.VMEM((TP, 48, TOK), F32),
            pltpu.VMEM((PAIRS, STATE, TOK), BF16),
            pltpu.VMEM((ROW, STATE, TOK), BF16),
            pltpu.VMEM((PAIRS, 1, TOK), F32),
            pltpu.VMEM((ROW, 1, TOK), F32),
            pltpu.VMEM((24, TOK), F32),
            pltpu.VMEM((ROWS - 1, 24, TOK), F32),
            pltpu.VMEM((ROW, STATE, TOK), F32),
            pltpu.VMEM((PAIRS, STATE, TOK), F32),
            pltpu.VMEM((TOK, 1024), F32),
            pltpu.VMEM((TOK, 1024), F32),
            pltpu.VMEM((8, TOK), F32),
            pltpu.VMEM((TP, 8, TOK), F32),
            pltpu.VMEM((ROW, STATE, TOK), F32),
            pltpu.SemaphoreType.DMA((11,)),
            pltpu.SemaphoreType.DMA((2,)),
            pltpu.SemaphoreType.DMA((2, 2, 8)),
            pltpu.SemaphoreType.DMA((3,)),
            pltpu.SemaphoreType.DMA((3,)),
            pltpu.SemaphoreType.DMA((3,)),
            pltpu.SemaphoreType.DMA((3,)),
            pltpu.SemaphoreType.DMA((3,)),
            pltpu.SemaphoreType.DMA((3,)),
            pltpu.SemaphoreType.DMA((3,)),
            pltpu.SemaphoreType.DMA((3,)),
            pltpu.SemaphoreType.DMA((6,)),
            pltpu.SemaphoreType.DMA((6,)),
            pltpu.SemaphoreType.REGULAR((3,)),
        ],
        compiler_params=pltpu.CompilerParams(
            collective_id=0, has_side_effects=True, vmem_limit_bytes=48 << 20
        ),
    )(*[pltpu.with_memory_space_constraint(a, pltpu.HBM) for a in (
        queries, keys, values, mixer_input, gate, step_weight, state_weight.T, step_bias,
        decay_rate, skip_gain, norm_gain.reshape(1, -1),
    )])


def solution(mesh):
    return jax.shard_map(
        per_device,
        mesh=mesh,
        in_specs=(P("ctx", "tp"),) * 5 + (P("tp", None),) * 2 + (P("tp"),) * 4,
        out_specs=(P("ctx", "tp"), P("ctx", "tp")),
        check_vma=False,
    )
```

```python
import functools
import math

import jax
import jax.numpy as jnp
from jax import lax
from jax.experimental import pallas as pl
from jax.experimental.pallas import tpu as pltpu
from jax.sharding import PartitionSpec as P

HD = 128
TOK = 128
ROW = 16
ROWS = 4
TP = 8
HEADS = 16
STATE = 16
PAIRS = 8
CHANNELS = 8192
SCALE2 = math.log2(math.e) / math.sqrt(HD)
F32 = jnp.float32
BF16 = jnp.bfloat16
EXACT = lax.Precision.HIGHEST
MESH = pl.DeviceIdType.MESH


SLOTS = (-2, -1, 0, 1, 2, 3, 4, -3, -4, 5, 6, -5, -6, 7, -7, -8)
PARTS = ((0, 5), (5, 9), (9, 13), (13, 16))


def slot_of(r):
    return SLOTS.index(r)


def dot(a, b, precision=None):
    return jnp.dot(a, b, preferred_element_type=F32, precision=precision)


def dot_t(a, b, precision=None):
    return lax.dot_general(
        a, b, (((1,), (1,)), ((), ())), preferred_element_type=F32, precision=precision
    )


def kernel(
    q_hbm, k_hbm, v_hbm, x_hbm, gate_hbm, ws_hbm, wm_hbm, bias_hbm, rate_hbm, skip_hbm, norm_hbm,
    attn_ref, mamba_ref,
    q_ref, x_ref, gate_ref, ws_ref, wm_ref, bias_ref, rate_ref, skip_ref, norm_ref,
    kbuf, vbuf, qbuf, obuf, orecv, stat_send, stat_recv, part, part_stat,
    proj_send, proj_recv, csend, crecv, fsend, frecv, ysend, yrecv, rsend, srecv,
    base, gated, sqsend, sqrecv, pref,
    load_sem, ring_ss, ring_rs, q_ss, q_rs, o_ss, o_rs, st_ss, st_rs, y_ss, y_rs, grp_ss, grp_rs, known,
):
    me = lax.axis_index("ctx")
    t = lax.axis_index("tp")
    y, z = me // ROW, me % ROW

    def tp_peer(o):
        return lax.rem(t + o, TP)

    def z_peer(o):
        return y * ROW + lax.rem(z + o + ROW, ROW)

    def y_peer(o):
        return lax.rem(y + o + ROWS, ROWS) * ROW + z

    def at(ctx, tp):
        return {"ctx": ctx, "tp": tp}

    def signal(sem, ctx, tp):
        pl.semaphore_signal(sem, inc=1, device_id=at(ctx, tp), device_id_type=MESH)

    barrier = pltpu.get_barrier_semaphore()
    for o in range(1, TP):
        signal(barrier, me, tp_peer(o))
    for o in (1, -1, 2, -2):
        signal(barrier, z_peer(o), t)
    for o in range(1, ROWS):
        signal(barrier, y_peer(o), t)

    loads = [
        pltpu.make_async_copy(src, dst, load_sem.at[i])
        for i, (src, dst) in enumerate((
            (x_hbm, x_ref), (ws_hbm, ws_ref), (wm_hbm, wm_ref), (bias_hbm, bias_ref),
            (rate_hbm, rate_ref), (skip_hbm, skip_ref), (k_hbm, kbuf.at[slot_of(0)]), (v_hbm, vbuf.at[slot_of(0)]),
            (q_hbm, q_ref), (gate_hbm, gate_ref), (norm_hbm, norm_ref),
        ))
    ]
    for copy in loads:
        copy.start()

    def remote(src, dst, ssem, rsem, ctx, tp):
        return pltpu.make_async_remote_copy(
            src_ref=src, dst_ref=dst, send_sem=ssem, recv_sem=rsem,
            device_id=at(ctx, tp), device_id_type=MESH,
        )

    for copy in loads[:6]:
        copy.wait()
    step_part = dot(x_ref[...], ws_ref[...]).T
    maps_part = dot_t(wm_ref[...], x_ref[...])
    for p in range(TP):
        proj_send[p, 0:16, :] = step_part[16 * p:16 * p + 16]
        proj_send[p, 16:48, :] = maps_part

    pl.semaphore_wait(barrier, TP - 1 + 4 + ROWS - 1)

    def proj_copy(o):
        return remote(
            proj_send.at[tp_peer(o)], proj_recv.at[t], grp_ss.at[0], grp_rs.at[0], me, tp_peer(o)
        )

    for o in (4, 3, 5, 2, 6, 1, 7):
        proj_copy(o).start()

    def ring_copy(kv, d, k):
        buf = (kbuf, vbuf)[kv]
        i = 0 if d > 0 else 1
        start = (k - 1) // 2 * 2
        src = buf.at[slot_of(-d * start)] if start else (k_hbm, v_hbm)[kv]
        return remote(
            src, buf.at[slot_of(-d * k)], ring_ss.at[kv], ring_rs.at[kv, i, k - 1],
            z_peer(d * (k - start)), t,
        )

    def reach(d):
        return ROW // 2 if d > 0 else ROW // 2 - 1

    pieces = [(kv, d) for kv in (0, 1) for d in (1, -1)]

    def ring_send(kv, d, start):
        for k in (start + 2, start + 1):
            if k <= reach(d):
                ring_copy(kv, d, k).start()

    for kv, d in pieces:
        ring_send(kv, d, 0)
    for o in (2, -2):
        signal(known.at[0], z_peer(o), t)

    def ring(stage):
        for kv, d in pieces:
            if 2 * stage <= reach(d):
                ring_copy(kv, d, 2 * stage).wait_recv()
                ring_send(kv, d, 2 * stage)
        for kv, d in pieces:
            ring_copy(kv, d, 2 * stage - 1).wait_recv()

    def q_copy(o):
        return remote(q_hbm, qbuf.at[o - 1], q_ss.at[o - 1], q_rs.at[o - 1], y_peer(-o), t)

    for o in range(1, ROWS):
        @pl.when(y >= o)
        def _(o=o):
            q_copy(o).start()

    lane = lax.broadcasted_iota(jnp.int32, (TOK, TOK), 1)
    sub = lax.broadcasted_iota(jnp.int32, (TOK, TOK), 0)
    low = lane < 64
    sub16 = lax.broadcasted_iota(jnp.int32, (HEADS, TOK), 0)
    lane16 = lax.broadcasted_iota(jnp.int32, (HEADS, TOK), 1)

    def column(ref):
        out = jnp.full((HEADS, TOK), ref[0], F32)
        for h in range(1, HEADS):
            out = jnp.where(sub16 == h, ref[h], out)
        return out

    bias, rate = column(bias_ref), column(rate_ref)

    def greet_far():
        pl.semaphore_wait(known.at[0], 2)
        for o in (4, -4):
            signal(known.at[1], z_peer(o), t)

    pl.when(z >= 6)(greet_far)
    ring(1)
    remote(
        proj_send.at[0:TP - 1], proj_recv.at[0:TP - 1], grp_ss.at[0], grp_rs.at[0], me, tp_peer(1)
    ).wait_recv()
    proj_recv[t] = proj_send[t]
    total = proj_recv[0]
    for p in range(1, TP):
        total = total + proj_recv[p]
    b_rows, c_rows = total[16:32], total[32:48]
    raw = total[0:16] + bias
    step = jnp.maximum(raw, 0.0) + jnp.log1p(jnp.exp(-jnp.abs(raw)))
    climb = -rate * step
    for sh in (1, 2, 4, 8, 16, 32, 64):
        climb = climb + jnp.where(lane16 >= sh, pltpu.roll(climb, sh, axis=1), 0.0)
    final = jnp.broadcast_to(climb[:, TOK - 1:TOK], (HEADS, TOK))
    for j in range(PAIRS):
        fsend[j] = jnp.where(low[0:1], final[2 * j:2 * j + 1], final[2 * j + 1:2 * j + 2])
    feed_weight = jnp.exp(final - climb) * step

    def pair_input(j):
        xp = x_ref[:, 128 * j:128 * j + 128]
        zero = jnp.zeros_like(xp)
        return jnp.concatenate([jnp.where(low, xp, zero), jnp.where(low, zero, xp)], axis=0)

    for j in range(PAIRS):
        feed = jnp.concatenate(
            [b_rows * feed_weight[h:h + 1] for h in (2 * j, 2 * j + 1)], axis=1
        ).astype(BF16)
        csend[j] = dot(feed, pair_input(j)).astype(BF16)

    pl.when(z < 6)(greet_far)
    pl.semaphore_wait(known.at[1], 2)

    def f_copy(o):
        return remote(
            fsend.at[lax.rem(z + o, PAIRS)], frecv.at[z], grp_ss.at[1], grp_rs.at[1],
            z_peer(o), t,
        )

    def c_copy(o):
        return remote(
            csend.at[lax.rem(z + o, PAIRS)], crecv.at[z], grp_ss.at[2], grp_rs.at[2], z_peer(o), t
        )

    for o in (8, 7, 9, 6, 10, 5, 11, 4, 12, 3, 13, 2, 14, 1, 15):
        f_copy(o).start()
        c_copy(o).start()
    crecv[z] = csend[lax.rem(z, PAIRS)]
    frecv[z] = fsend[lax.rem(z, PAIRS)]
    turned = jnp.concatenate([c_rows, climb, jnp.exp(climb), jnp.zeros((80, TOK), F32)], axis=0).T
    c_cols = turned[:, 0:16]
    inner = dot(c_cols, b_rows, EXACT)
    causal = sub >= lane

    def local_pair(j):
        mixes = []
        for h in (2 * j, 2 * j + 1):
            diff = turned[:, 16 + h:17 + h] - climb[h:h + 1]
            mix = inner * jnp.exp(diff) * step[h:h + 1]
            mixes.append(jnp.where(causal, mix, 0.0).astype(BF16))
        out = dot(jnp.concatenate(mixes, axis=1), pair_input(j))
        gain = jnp.where(low, skip_ref[2 * j], skip_ref[2 * j + 1])
        cols = slice(128 * j, 128 * j + 128)
        base[:, cols] = out + gain * x_ref[:, cols].astype(F32)

    for j in range(PAIRS):
        local_pair(j)

    query_row = lax.broadcasted_iota(jnp.int32, (4 * TOK, 1), 0) % TOK + z * TOK

    def attend(o, number):
        first, last = PARTS[number]
        src = q_ref if o == 0 else qbuf.at[o - 1]
        q = jnp.concatenate([src[:, 128 * h:128 * h + 128] for h in range(4)], axis=0)
        width = (last - first) * TOK
        scores = dot_t(q, kbuf[first:last].reshape(width, HD))
        blocks = [scores[:, TOK * i:TOK * i + TOK] for i in range(last - first)]
        if o == 0:
            place = lax.broadcasted_iota(jnp.int32, (1, TOK), 1)
            blocks = [
                jnp.where(
                    place + lax.rem(z + SLOTS[first + i] + ROW, ROW) * TOK <= query_row, b, -1e30
                )
                for i, b in enumerate(blocks)
            ]
        top = blocks[0]
        for b in blocks[1:]:
            top = jnp.maximum(top, b)
        top = jnp.broadcast_to(jnp.max(top, axis=1, keepdims=True), (4 * TOK, TOK))
        if number:
            before = part_stat[o]
            top = jnp.maximum(before, top)
        weights = jnp.concatenate(
            [jnp.exp2((b - top) * SCALE2).astype(BF16) for b in blocks], axis=1
        )
        held = vbuf[first:last].reshape(width, HD)
        mixed = dot(weights, jnp.concatenate([held, jnp.ones_like(held)], axis=1))
        if number:
            keep = jnp.exp2((before - top) * SCALE2)
            mixed = mixed + part[o] * jnp.concatenate([keep, keep], axis=1)
        if number == 3 and o:
            whole = mixed[:, HD:]
            obuf[o - 1] = (mixed[:, 0:HD] / whole).astype(BF16)
            stats = jnp.zeros((TOK, TOK), F32)
            for h in range(4):
                rows = slice(TOK * h, TOK * h + TOK)
                stats = jnp.where(lane == h, top[rows], stats)
                stats = jnp.where(lane == 4 + h, whole[rows], stats)
            stat_send[o - 1] = stats.T[0:8]
            return
        part[o] = mixed
        part_stat[o] = top

    def attend_some(number, *queries):
        for row in range(ROWS):
            mine = [o for o in queries if row + o < ROWS]
            if mine:
                @pl.when(y == row)
                def _(mine=mine):
                    if not number:
                        for o in mine:
                            if o:
                                q_copy(o).wait_recv()
                    for o in mine:
                        attend(o, number)

    for copy in loads[6:]:
        copy.wait()
    attend_some(0, 1, 2, 3, 0)
    ring(2)
    attend_some(1, 1, 2, 3, 0)
    remote(
        frecv.at[0:ROW - 1], frecv.at[0:ROW - 1], grp_ss.at[1], grp_rs.at[1], z_peer(1), t
    ).wait_recv()
    remote(
        crecv.at[0:ROW - 1], crecv.at[0:ROW - 1], grp_ss.at[2], grp_rs.at[2], z_peer(1), t
    ).wait_recv()
    running = jnp.zeros((STATE, TOK), F32)
    passed = jnp.zeros((1, TOK), F32)
    gone = []
    for b in range(ROW):
        pref[b] = running
        gone.append(passed)
        running = jnp.exp(frecv[b]) * running + crecv[b].astype(F32)
        passed = passed + frecv[b]
    ysend[0:16] = running
    ysend[16:24] = jnp.broadcast_to(passed, (8, TOK))

    def y_copy(o):
        return remote(ysend, yrecv.at[o - 1], y_ss.at[o - 1], y_rs.at[o - 1], y_peer(o), t)

    for o in range(1, ROWS):
        @pl.when(y + o < ROWS)
        def _(o=o):
            y_copy(o).start()

    ring(3)
    for o in range(1, ROWS):
        @pl.when(y >= o)
        def _(o=o):
            y_copy(o).wait_recv()

        @pl.when(y < o)
        def _(o=o):
            yrecv[o - 1] = jnp.zeros((24, TOK), F32)

    enter = jnp.zeros((STATE, TOK), F32)
    for o in (3, 2, 1):
        enter = jnp.exp(yrecv[o - 1, 16:17]) * enter + yrecv[o - 1, 0:16]
    for b in range(ROW):
        rsend[b] = pref[b] + jnp.exp(gone[b]) * enter

    def r_copy(o):
        return remote(
            rsend.at[lax.rem(z + o + ROW, ROW)], srecv.at[lax.rem(z, PAIRS)],
            grp_ss.at[4], grp_rs.at[4], z_peer(o), t,
        )

    for o in (-4, 3, -3, 2, -2, 1, -1):
        r_copy(o).start()
    srecv[lax.rem(z, PAIRS)] = rsend[z]
    attend_some(2, 1, 2, 3, 0)
    ring(4)
    def o_copy(o):
        return remote(
            obuf.at[o - 1], orecv.at[o - 1], o_ss.at[o - 1], o_rs.at[o - 1], y_peer(o), t
        )

    def st_copy(o):
        return remote(
            stat_send.at[o - 1], stat_recv.at[o - 1], st_ss.at[o - 1], st_rs.at[o - 1],
            y_peer(o), t,
        )

    attend_some(3, 3, 2, 1)
    for o in (3, 2, 1):
        @pl.when(y + o < ROWS)
        def _(o=o):
            o_copy(o).start()
            st_copy(o).start()

    remote(
        srecv.at[0:PAIRS - 1], srecv.at[0:PAIRS - 1], grp_ss.at[4], grp_rs.at[4], z_peer(1), t
    ).wait_recv()
    squares = jnp.zeros((TOK, TOK), F32)
    for j in range(PAIRS):
        cols = slice(128 * j, 128 * j + 128)
        state = srecv[j]
        grown = jnp.where(low, turned[:, 32 + 2 * j:33 + 2 * j], turned[:, 33 + 2 * j:34 + 2 * j])
        out = base[:, cols] + grown * dot(c_cols, state, EXACT)
        g = gate_ref[:, cols].astype(F32)
        out = out * (g / (1.0 + jnp.exp(-g)))
        gated[:, cols] = out
        squares = squares + out * out
    sqsend[...] = dot_t(jnp.ones((8, TOK), F32), squares, EXACT)

    def sq_copy(o):
        return remote(sqsend, sqrecv.at[t], grp_ss.at[5], grp_rs.at[5], me, tp_peer(o))

    for o in range(1, TP):
        sq_copy(o).start()
    sqrecv[t] = sqsend[...]

    attend(0, 3)
    for o in range(1, ROWS):
        @pl.when(y >= o)
        def _(o=o):
            st_copy(o).wait_recv()
            o_copy(o).wait_recv()
            other = jnp.concatenate([stat_recv[o - 1], jnp.zeros((120, TOK), F32)], axis=0).T
            for h in range(4):
                rows = slice(TOK * h, TOK * h + TOK)
                before, theirs = part_stat[0, rows], other[:, h:h + 1]
                top = jnp.maximum(before, theirs)
                keep = jnp.exp2((before - top) * SCALE2)
                gain = other[:, 4 + h:5 + h] * jnp.exp2((theirs - top) * SCALE2)
                part[0, rows, 0:HD] = (
                    part[0, rows, 0:HD] * keep + orecv[o - 1, rows].astype(F32) * gain
                )
                part[0, rows, HD:] = part[0, rows, HD:] * keep + gain
                part_stat[0, rows] = top

    for h in range(4):
        rows = slice(TOK * h, TOK * h + TOK)
        attn_ref[:, rows] = (part[0, rows, 0:HD] / part[0, rows, HD:]).astype(BF16)

    remote(
        sqrecv.at[0:TP - 1], sqrecv.at[0:TP - 1], grp_ss.at[5], grp_rs.at[5], me, tp_peer(1)
    ).wait_recv()
    square = sqrecv[0]
    for p in range(1, TP):
        square = square + sqrecv[p]
    inverse = lax.rsqrt(square[0:1] / CHANNELS + 1e-5)
    inverse = jnp.broadcast_to(inverse, (TOK, TOK)).T
    for j in range(PAIRS):
        cols = slice(128 * j, 128 * j + 128)
        mamba_ref[:, cols] = (gated[:, cols] * inverse * norm_ref[0:1, cols]).astype(BF16)

    remote(
        proj_send.at[0:TP - 1], proj_recv.at[0:TP - 1], grp_ss.at[0], grp_rs.at[0], me, tp_peer(1)
    ).wait_send()
    remote(
        frecv.at[0:ROW - 1], frecv.at[0:ROW - 1], grp_ss.at[1], grp_rs.at[1], z_peer(1), t
    ).wait_send()
    remote(
        crecv.at[0:ROW - 1], crecv.at[0:ROW - 1], grp_ss.at[2], grp_rs.at[2], z_peer(1), t
    ).wait_send()
    remote(
        srecv.at[0:PAIRS - 1], srecv.at[0:PAIRS - 1], grp_ss.at[4], grp_rs.at[4], z_peer(1), t
    ).wait_send()
    remote(
        sqrecv.at[0:TP - 1], sqrecv.at[0:TP - 1], grp_ss.at[5], grp_rs.at[5], me, tp_peer(1)
    ).wait_send()
    for kv, buf in ((0, kbuf), (1, vbuf)):
        remote(
            buf.at[0:ROW - 1], buf.at[0:ROW - 1], ring_ss.at[kv], ring_rs.at[kv, 0, 0], z_peer(1), t
        ).wait_send()
    for o in range(1, ROWS):
        @pl.when(y >= o)
        def _(o=o):
            q_copy(o).wait_send()

        @pl.when(y + o < ROWS)
        def _(o=o):
            o_copy(o).wait_send()
            y_copy(o).wait_send()
            st_copy(o).wait_send()


def per_device(
    queries, keys, values, mixer_input, gate, step_weight, state_weight, step_bias, decay_rate,
    skip_gain, norm_gain,
):
    vmem = pl.BlockSpec(memory_space=pltpu.VMEM)
    hbm = pl.BlockSpec(memory_space=pltpu.HBM)
    return pl.pallas_call(
        kernel,
        out_shape=(
            jax.ShapeDtypeStruct((TOK, 4 * HD), BF16),
            jax.ShapeDtypeStruct((TOK, 1024), BF16),
        ),
        in_specs=[hbm] * 11,
        out_specs=(vmem, vmem),
        scratch_shapes=[
            pltpu.VMEM((TOK, 4 * HD), BF16),
            pltpu.VMEM((TOK, 1024), BF16),
            pltpu.VMEM((TOK, 1024), BF16),
            pltpu.VMEM((1024, 128), BF16),
            pltpu.VMEM((32, 1024), BF16),
            pltpu.SMEM((HEADS,), F32),
            pltpu.SMEM((HEADS,), F32),
            pltpu.SMEM((HEADS,), F32),
            pltpu.VMEM((1, 1024), F32),
            pltpu.VMEM((ROW, TOK, HD), BF16),
            pltpu.VMEM((ROW, TOK, HD), BF16),
            pltpu.VMEM((3, TOK, 4 * HD), BF16),
            pltpu.VMEM((3, 4 * TOK, HD), BF16),
            pltpu.VMEM((3, 4 * TOK, HD), BF16),
            pltpu.VMEM((3, 8, TOK), F32),
            pltpu.VMEM((3, 8, TOK), F32),
            pltpu.VMEM((4, 4 * TOK, 2 * HD), F32),
            pltpu.VMEM((4, 4 * TOK, TOK), F32),
            pltpu.VMEM((TP, 48, TOK), F32),
            pltpu.VMEM((TP, 48, TOK), F32),
            pltpu.VMEM((PAIRS, STATE, TOK), BF16),
            pltpu.VMEM((ROW, STATE, TOK), BF16),
            pltpu.VMEM((PAIRS, 1, TOK), F32),
            pltpu.VMEM((ROW, 1, TOK), F32),
            pltpu.VMEM((24, TOK), F32),
            pltpu.VMEM((ROWS - 1, 24, TOK), F32),
            pltpu.VMEM((ROW, STATE, TOK), F32),
            pltpu.VMEM((PAIRS, STATE, TOK), F32),
            pltpu.VMEM((TOK, 1024), F32),
            pltpu.VMEM((TOK, 1024), F32),
            pltpu.VMEM((8, TOK), F32),
            pltpu.VMEM((TP, 8, TOK), F32),
            pltpu.VMEM((ROW, STATE, TOK), F32),
            pltpu.SemaphoreType.DMA((11,)),
            pltpu.SemaphoreType.DMA((2,)),
            pltpu.SemaphoreType.DMA((2, 2, 8)),
            pltpu.SemaphoreType.DMA((3,)),
            pltpu.SemaphoreType.DMA((3,)),
            pltpu.SemaphoreType.DMA((3,)),
            pltpu.SemaphoreType.DMA((3,)),
            pltpu.SemaphoreType.DMA((3,)),
            pltpu.SemaphoreType.DMA((3,)),
            pltpu.SemaphoreType.DMA((3,)),
            pltpu.SemaphoreType.DMA((3,)),
            pltpu.SemaphoreType.DMA((6,)),
            pltpu.SemaphoreType.DMA((6,)),
            pltpu.SemaphoreType.REGULAR((2,)),
        ],
        compiler_params=pltpu.CompilerParams(
            collective_id=0, has_side_effects=True, vmem_limit_bytes=48 << 20
        ),
    )(*[pltpu.with_memory_space_constraint(a, pltpu.HBM) for a in (
        queries, keys, values, mixer_input, gate, step_weight, state_weight.T, step_bias,
        decay_rate, skip_gain, norm_gain.reshape(1, -1),
    )])


def solution(mesh):
    return jax.shard_map(
        per_device,
        mesh=mesh,
        in_specs=(P("ctx", "tp"),) * 5 + (P("tp", None),) * 2 + (P("tp"),) * 4,
        out_specs=(P("ctx", "tp"), P("ctx", "tp")),
        check_vma=False,
    )
```

```python
import functools
import math

import jax
import jax.numpy as jnp
from jax import lax
from jax.experimental import pallas as pl
from jax.experimental.pallas import tpu as pltpu
from jax.sharding import PartitionSpec as P

HD = 128
TOK = 128
ROW = 16
ROWS = 4
TP = 8
HEADS = 16
STATE = 16
PAIRS = 8
CHANNELS = 8192
SCALE2 = math.log2(math.e) / math.sqrt(HD)
F32 = jnp.float32
BF16 = jnp.bfloat16
EXACT = lax.Precision.HIGHEST
MESH = pl.DeviceIdType.MESH


SLOTS = (-2, -1, 0, 1, 2, 3, 4, -3, -4, 5, 6, -5, -6, 7, -7, -8)
PARTS = ((0, 5), (5, 9), (9, 13), (13, 16))


def slot_of(r):
    return SLOTS.index(r)


def dot(a, b, precision=None):
    return jnp.dot(a, b, preferred_element_type=F32, precision=precision)


def dot_t(a, b, precision=None):
    return lax.dot_general(
        a, b, (((1,), (1,)), ((), ())), preferred_element_type=F32, precision=precision
    )


def kernel(
    q_hbm, k_hbm, v_hbm, x_hbm, gate_hbm, ws_hbm, wm_hbm, bias_hbm, rate_hbm, skip_hbm, norm_hbm,
    attn_ref, mamba_ref,
    q_ref, x_ref, gate_ref, ws_ref, wm_ref, bias_ref, rate_ref, skip_ref, norm_ref,
    kbuf, vbuf, qbuf, obuf, orecv, stat_send, stat_recv, part, part_stat,
    proj_send, proj_recv, csend, crecv, fsend, frecv, ysend, yrecv, rsend, srecv,
    base, gated, sqsend, sqrecv, pref,
    load_sem, ring_ss, ring_rs, q_ss, q_rs, o_ss, o_rs, st_ss, st_rs, y_ss, y_rs, grp_ss, grp_rs, known,
):
    me = lax.axis_index("ctx")
    t = lax.axis_index("tp")
    y, z = me // ROW, me % ROW

    def tp_peer(o):
        return lax.rem(t + o, TP)

    def z_peer(o):
        return y * ROW + lax.rem(z + o + ROW, ROW)

    def y_peer(o):
        return lax.rem(y + o + ROWS, ROWS) * ROW + z

    def at(ctx, tp):
        return {"ctx": ctx, "tp": tp}

    def signal(sem, ctx, tp):
        pl.semaphore_signal(sem, inc=1, device_id=at(ctx, tp), device_id_type=MESH)

    barrier = pltpu.get_barrier_semaphore()
    for o in range(1, TP):
        signal(barrier, me, tp_peer(o))
    for o in (1, -1, 2, -2):
        signal(barrier, z_peer(o), t)
    for o in range(1, ROWS):
        signal(barrier, y_peer(o), t)

    loads = [
        pltpu.make_async_copy(src, dst, load_sem.at[i])
        for i, (src, dst) in enumerate((
            (x_hbm, x_ref), (ws_hbm, ws_ref), (wm_hbm, wm_ref), (bias_hbm, bias_ref),
            (rate_hbm, rate_ref), (skip_hbm, skip_ref), (k_hbm, kbuf.at[slot_of(0)]), (v_hbm, vbuf.at[slot_of(0)]),
            (q_hbm, q_ref), (gate_hbm, gate_ref), (norm_hbm, norm_ref),
        ))
    ]
    for copy in loads:
        copy.start()

    def remote(src, dst, ssem, rsem, ctx, tp):
        return pltpu.make_async_remote_copy(
            src_ref=src, dst_ref=dst, send_sem=ssem, recv_sem=rsem,
            device_id=at(ctx, tp), device_id_type=MESH,
        )

    for copy in loads[:6]:
        copy.wait()
    step_part = dot(x_ref[...], ws_ref[...]).T
    maps_part = dot_t(wm_ref[...], x_ref[...])
    for p in range(TP):
        proj_send[p, 0:16, :] = step_part[16 * p:16 * p + 16]
        proj_send[p, 16:48, :] = maps_part

    pl.semaphore_wait(barrier, TP - 1 + 4 + ROWS - 1)

    def proj_copy(o):
        return remote(
            proj_send.at[tp_peer(o)], proj_recv.at[t], grp_ss.at[0], grp_rs.at[0], me, tp_peer(o)
        )

    for o in (4, 3, 5, 2, 6, 1, 7):
        proj_copy(o).start()

    def ring_copy(kv, d, k):
        buf = (kbuf, vbuf)[kv]
        i = 0 if d > 0 else 1
        start = (k - 1) // 2 * 2
        src = buf.at[slot_of(-d * start)] if start else (k_hbm, v_hbm)[kv]
        return remote(
            src, buf.at[slot_of(-d * k)], ring_ss.at[kv], ring_rs.at[kv, i, k - 1],
            z_peer(d * (k - start)), t,
        )

    def reach(d):
        return ROW // 2 if d > 0 else ROW // 2 - 1

    pieces = [(kv, d) for kv in (0, 1) for d in (1, -1)]

    def ring_send(kv, d, k):
        if k <= reach(d):
            ring_copy(kv, d, k).start()

    for k in (2, 1):
        for kv, d in pieces:
            ring_send(kv, d, k)
    for o in (2, -2):
        signal(known.at[0], z_peer(o), t)

    def ring(stage):
        for kv, d in pieces:
            if 2 * stage <= reach(d):
                ring_copy(kv, d, 2 * stage).wait_recv()
                ring_send(kv, d, 2 * stage + 2)
        for kv, d in pieces:
            ring_send(kv, d, 2 * stage + 1)
        for kv, d in pieces:
            ring_copy(kv, d, 2 * stage - 1).wait_recv()

    def q_copy(o):
        return remote(q_hbm, qbuf.at[o - 1], q_ss.at[o - 1], q_rs.at[o - 1], y_peer(-o), t)

    for o in range(1, ROWS):
        @pl.when(y >= o)
        def _(o=o):
            q_copy(o).start()

    lane = lax.broadcasted_iota(jnp.int32, (TOK, TOK), 1)
    sub = lax.broadcasted_iota(jnp.int32, (TOK, TOK), 0)
    low = lane < 64
    sub16 = lax.broadcasted_iota(jnp.int32, (HEADS, TOK), 0)
    lane16 = lax.broadcasted_iota(jnp.int32, (HEADS, TOK), 1)

    def column(ref):
        out = jnp.full((HEADS, TOK), ref[0], F32)
        for h in range(1, HEADS):
            out = jnp.where(sub16 == h, ref[h], out)
        return out

    bias, rate = column(bias_ref), column(rate_ref)

    def greet_far():
        pl.semaphore_wait(known.at[0], 2)
        for o in (4, -4):
            signal(known.at[1], z_peer(o), t)

    pl.when(z >= 6)(greet_far)
    ring(1)
    remote(
        proj_send.at[0:TP - 1], proj_recv.at[0:TP - 1], grp_ss.at[0], grp_rs.at[0], me, tp_peer(1)
    ).wait_recv()
    proj_recv[t] = proj_send[t]
    total = proj_recv[0]
    for p in range(1, TP):
        total = total + proj_recv[p]
    b_rows, c_rows = total[16:32], total[32:48]
    raw = total[0:16] + bias
    step = jnp.maximum(raw, 0.0) + jnp.log1p(jnp.exp(-jnp.abs(raw)))
    climb = -rate * step
    for sh in (1, 2, 4, 8, 16, 32, 64):
        climb = climb + jnp.where(lane16 >= sh, pltpu.roll(climb, sh, axis=1), 0.0)
    final = jnp.broadcast_to(climb[:, TOK - 1:TOK], (HEADS, TOK))
    for j in range(PAIRS):
        fsend[j] = jnp.where(low[0:1], final[2 * j:2 * j + 1], final[2 * j + 1:2 * j + 2])
    feed_weight = jnp.exp(final - climb) * step

    def pair_input(j):
        xp = x_ref[:, 128 * j:128 * j + 128]
        zero = jnp.zeros_like(xp)
        return jnp.concatenate([jnp.where(low, xp, zero), jnp.where(low, zero, xp)], axis=0)

    for j in range(PAIRS):
        feed = jnp.concatenate(
            [b_rows * feed_weight[h:h + 1] for h in (2 * j, 2 * j + 1)], axis=1
        ).astype(BF16)
        csend[j] = dot(feed, pair_input(j)).astype(BF16)

    pl.when(z < 6)(greet_far)
    pl.semaphore_wait(known.at[1], 2)

    def f_copy(o):
        return remote(
            fsend.at[lax.rem(z + o, PAIRS)], frecv.at[z], grp_ss.at[1], grp_rs.at[1],
            z_peer(o), t,
        )

    def c_copy(o):
        return remote(
            csend.at[lax.rem(z + o, PAIRS)], crecv.at[z], grp_ss.at[2], grp_rs.at[2], z_peer(o), t
        )

    for o in (8, 7, 9, 6, 10, 5, 11, 4, 12, 3, 13, 2, 14, 1, 15):
        f_copy(o).start()
        c_copy(o).start()
    crecv[z] = csend[lax.rem(z, PAIRS)]
    frecv[z] = fsend[lax.rem(z, PAIRS)]
    turned = jnp.concatenate([c_rows, climb, jnp.exp(climb), jnp.zeros((80, TOK), F32)], axis=0).T
    c_cols = turned[:, 0:16]
    inner = dot(c_cols, b_rows, EXACT)
    causal = sub >= lane

    def local_pair(j):
        mixes = []
        for h in (2 * j, 2 * j + 1):
            diff = turned[:, 16 + h:17 + h] - climb[h:h + 1]
            mix = inner * jnp.exp(diff) * step[h:h + 1]
            mixes.append(jnp.where(causal, mix, 0.0).astype(BF16))
        out = dot(jnp.concatenate(mixes, axis=1), pair_input(j))
        gain = jnp.where(low, skip_ref[2 * j], skip_ref[2 * j + 1])
        cols = slice(128 * j, 128 * j + 128)
        base[:, cols] = out + gain * x_ref[:, cols].astype(F32)

    for j in range(PAIRS):
        local_pair(j)

    query_row = lax.broadcasted_iota(jnp.int32, (4 * TOK, 1), 0) % TOK + z * TOK

    def attend(o, number):
        first, last = PARTS[number]
        src = q_ref if o == 0 else qbuf.at[o - 1]
        q = jnp.concatenate([src[:, 128 * h:128 * h + 128] for h in range(4)], axis=0)
        width = (last - first) * TOK
        scores = dot_t(q, kbuf[first:last].reshape(width, HD))
        blocks = [scores[:, TOK * i:TOK * i + TOK] for i in range(last - first)]
        if o == 0:
            place = lax.broadcasted_iota(jnp.int32, (1, TOK), 1)
            blocks = [
                jnp.where(
                    place + lax.rem(z + SLOTS[first + i] + ROW, ROW) * TOK <= query_row, b, -1e30
                )
                for i, b in enumerate(blocks)
            ]
        top = blocks[0]
        for b in blocks[1:]:
            top = jnp.maximum(top, b)
        top = jnp.broadcast_to(jnp.max(top, axis=1, keepdims=True), (4 * TOK, TOK))
        if number:
            before = part_stat[o]
            top = jnp.maximum(before, top)
        weights = jnp.concatenate(
            [jnp.exp2((b - top) * SCALE2).astype(BF16) for b in blocks], axis=1
        )
        held = vbuf[first:last].reshape(width, HD)
        mixed = dot(weights, jnp.concatenate([held, jnp.ones_like(held)], axis=1))
        if number:
            keep = jnp.exp2((before - top) * SCALE2)
            mixed = mixed + part[o] * jnp.concatenate([keep, keep], axis=1)
        if number == 3 and o:
            whole = mixed[:, HD:]
            obuf[o - 1] = (mixed[:, 0:HD] / whole).astype(BF16)
            stats = jnp.zeros((TOK, TOK), F32)
            for h in range(4):
                rows = slice(TOK * h, TOK * h + TOK)
                stats = jnp.where(lane == h, top[rows], stats)
                stats = jnp.where(lane == 4 + h, whole[rows], stats)
            stat_send[o - 1] = stats.T[0:8]
            return
        part[o] = mixed
        part_stat[o] = top

    def attend_some(number, *queries):
        for row in range(ROWS):
            mine = [o for o in queries if row + o < ROWS]
            if mine:
                @pl.when(y == row)
                def _(mine=mine):
                    if not number:
                        for o in mine:
                            if o:
                                q_copy(o).wait_recv()
                    for o in mine:
                        attend(o, number)

    for copy in loads[6:]:
        copy.wait()
    attend_some(0, 1, 2, 3, 0)
    ring(2)
    attend_some(1, 1, 2, 3, 0)
    remote(
        frecv.at[0:ROW - 1], frecv.at[0:ROW - 1], grp_ss.at[1], grp_rs.at[1], z_peer(1), t
    ).wait_recv()
    remote(
        crecv.at[0:ROW - 1], crecv.at[0:ROW - 1], grp_ss.at[2], grp_rs.at[2], z_peer(1), t
    ).wait_recv()
    running = jnp.zeros((STATE, TOK), F32)
    passed = jnp.zeros((1, TOK), F32)
    gone = []
    for b in range(ROW):
        pref[b] = running
        gone.append(passed)
        running = jnp.exp(frecv[b]) * running + crecv[b].astype(F32)
        passed = passed + frecv[b]
    ysend[0:16] = running
    ysend[16:24] = jnp.broadcast_to(passed, (8, TOK))

    def y_copy(o):
        return remote(ysend, yrecv.at[o - 1], y_ss.at[o - 1], y_rs.at[o - 1], y_peer(o), t)

    for o in range(1, ROWS):
        @pl.when(y + o < ROWS)
        def _(o=o):
            y_copy(o).start()

    ring(3)
    for o in range(1, ROWS):
        @pl.when(y >= o)
        def _(o=o):
            y_copy(o).wait_recv()

        @pl.when(y < o)
        def _(o=o):
            yrecv[o - 1] = jnp.zeros((24, TOK), F32)

    enter = jnp.zeros((STATE, TOK), F32)
    for o in (3, 2, 1):
        enter = jnp.exp(yrecv[o - 1, 16:17]) * enter + yrecv[o - 1, 0:16]
    for b in range(ROW):
        rsend[b] = pref[b] + jnp.exp(gone[b]) * enter

    def r_copy(o):
        return remote(
            rsend.at[lax.rem(z + o + ROW, ROW)], srecv.at[lax.rem(z, PAIRS)],
            grp_ss.at[4], grp_rs.at[4], z_peer(o), t,
        )

    for o in (-4, 3, -3, 2, -2, 1, -1):
        r_copy(o).start()
    srecv[lax.rem(z, PAIRS)] = rsend[z]
    attend_some(2, 1, 2, 3, 0)
    ring(4)
    def o_copy(o):
        return remote(
            obuf.at[o - 1], orecv.at[o - 1], o_ss.at[o - 1], o_rs.at[o - 1], y_peer(o), t
        )

    def st_copy(o):
        return remote(
            stat_send.at[o - 1], stat_recv.at[o - 1], st_ss.at[o - 1], st_rs.at[o - 1],
            y_peer(o), t,
        )

    attend_some(3, 3, 2, 1)
    for o in (3, 2, 1):
        @pl.when(y + o < ROWS)
        def _(o=o):
            o_copy(o).start()
            st_copy(o).start()

    remote(
        srecv.at[0:PAIRS - 1], srecv.at[0:PAIRS - 1], grp_ss.at[4], grp_rs.at[4], z_peer(1), t
    ).wait_recv()
    squares = jnp.zeros((TOK, TOK), F32)
    for j in range(PAIRS):
        cols = slice(128 * j, 128 * j + 128)
        state = srecv[j]
        grown = jnp.where(low, turned[:, 32 + 2 * j:33 + 2 * j], turned[:, 33 + 2 * j:34 + 2 * j])
        out = base[:, cols] + grown * dot(c_cols, state, EXACT)
        g = gate_ref[:, cols].astype(F32)
        out = out * (g / (1.0 + jnp.exp(-g)))
        gated[:, cols] = out
        squares = squares + out * out
    sqsend[...] = dot_t(jnp.ones((8, TOK), F32), squares, EXACT)

    def sq_copy(o):
        return remote(sqsend, sqrecv.at[t], grp_ss.at[5], grp_rs.at[5], me, tp_peer(o))

    for o in range(1, TP):
        sq_copy(o).start()
    sqrecv[t] = sqsend[...]

    attend(0, 3)
    for o in range(1, ROWS):
        @pl.when(y >= o)
        def _(o=o):
            st_copy(o).wait_recv()
            o_copy(o).wait_recv()
            other = jnp.concatenate([stat_recv[o - 1], jnp.zeros((120, TOK), F32)], axis=0).T
            for h in range(4):
                rows = slice(TOK * h, TOK * h + TOK)
                before, theirs = part_stat[0, rows], other[:, h:h + 1]
                top = jnp.maximum(before, theirs)
                keep = jnp.exp2((before - top) * SCALE2)
                gain = other[:, 4 + h:5 + h] * jnp.exp2((theirs - top) * SCALE2)
                part[0, rows, 0:HD] = (
                    part[0, rows, 0:HD] * keep + orecv[o - 1, rows].astype(F32) * gain
                )
                part[0, rows, HD:] = part[0, rows, HD:] * keep + gain
                part_stat[0, rows] = top

    for h in range(4):
        rows = slice(TOK * h, TOK * h + TOK)
        attn_ref[:, rows] = (part[0, rows, 0:HD] / part[0, rows, HD:]).astype(BF16)

    remote(
        sqrecv.at[0:TP - 1], sqrecv.at[0:TP - 1], grp_ss.at[5], grp_rs.at[5], me, tp_peer(1)
    ).wait_recv()
    square = sqrecv[0]
    for p in range(1, TP):
        square = square + sqrecv[p]
    inverse = lax.rsqrt(square[0:1] / CHANNELS + 1e-5)
    inverse = jnp.broadcast_to(inverse, (TOK, TOK)).T
    for j in range(PAIRS):
        cols = slice(128 * j, 128 * j + 128)
        mamba_ref[:, cols] = (gated[:, cols] * inverse * norm_ref[0:1, cols]).astype(BF16)

    remote(
        proj_send.at[0:TP - 1], proj_recv.at[0:TP - 1], grp_ss.at[0], grp_rs.at[0], me, tp_peer(1)
    ).wait_send()
    remote(
        frecv.at[0:ROW - 1], frecv.at[0:ROW - 1], grp_ss.at[1], grp_rs.at[1], z_peer(1), t
    ).wait_send()
    remote(
        crecv.at[0:ROW - 1], crecv.at[0:ROW - 1], grp_ss.at[2], grp_rs.at[2], z_peer(1), t
    ).wait_send()
    remote(
        srecv.at[0:PAIRS - 1], srecv.at[0:PAIRS - 1], grp_ss.at[4], grp_rs.at[4], z_peer(1), t
    ).wait_send()
    remote(
        sqrecv.at[0:TP - 1], sqrecv.at[0:TP - 1], grp_ss.at[5], grp_rs.at[5], me, tp_peer(1)
    ).wait_send()
    for kv, buf in ((0, kbuf), (1, vbuf)):
        remote(
            buf.at[0:ROW - 1], buf.at[0:ROW - 1], ring_ss.at[kv], ring_rs.at[kv, 0, 0], z_peer(1), t
        ).wait_send()
    for o in range(1, ROWS):
        @pl.when(y >= o)
        def _(o=o):
            q_copy(o).wait_send()

        @pl.when(y + o < ROWS)
        def _(o=o):
            o_copy(o).wait_send()
            y_copy(o).wait_send()
            st_copy(o).wait_send()


def write_out(attn, mamba, attn_hbm, mamba_hbm, sems):
    copies = [
        pltpu.make_async_copy(attn, attn_hbm, sems.at[0]),
        pltpu.make_async_copy(mamba, mamba_hbm, sems.at[1]),
    ]
    for copy in copies:
        copy.start()
    for copy in copies:
        copy.wait()


def per_device(
    queries, keys, values, mixer_input, gate, step_weight, state_weight, step_bias, decay_rate,
    skip_gain, norm_gain,
):
    vmem = pl.BlockSpec(memory_space=pltpu.VMEM)
    hbm = pl.BlockSpec(memory_space=pltpu.HBM)
    shapes = (
        jax.ShapeDtypeStruct((TOK, 4 * HD), BF16),
        jax.ShapeDtypeStruct((TOK, 1024), BF16),
    )
    results = pl.pallas_call(
        kernel,
        out_shape=shapes,
        in_specs=[hbm] * 11,
        out_specs=(vmem, vmem),
        scratch_shapes=[
            pltpu.VMEM((TOK, 4 * HD), BF16),
            pltpu.VMEM((TOK, 1024), BF16),
            pltpu.VMEM((TOK, 1024), BF16),
            pltpu.VMEM((1024, 128), BF16),
            pltpu.VMEM((32, 1024), BF16),
            pltpu.SMEM((HEADS,), F32),
            pltpu.SMEM((HEADS,), F32),
            pltpu.SMEM((HEADS,), F32),
            pltpu.VMEM((1, 1024), F32),
            pltpu.VMEM((ROW, TOK, HD), BF16),
            pltpu.VMEM((ROW, TOK, HD), BF16),
            pltpu.VMEM((3, TOK, 4 * HD), BF16),
            pltpu.VMEM((3, 4 * TOK, HD), BF16),
            pltpu.VMEM((3, 4 * TOK, HD), BF16),
            pltpu.VMEM((3, 8, TOK), F32),
            pltpu.VMEM((3, 8, TOK), F32),
            pltpu.VMEM((4, 4 * TOK, 2 * HD), F32),
            pltpu.VMEM((4, 4 * TOK, TOK), F32),
            pltpu.VMEM((TP, 48, TOK), F32),
            pltpu.VMEM((TP, 48, TOK), F32),
            pltpu.VMEM((PAIRS, STATE, TOK), BF16),
            pltpu.VMEM((ROW, STATE, TOK), BF16),
            pltpu.VMEM((PAIRS, 1, TOK), F32),
            pltpu.VMEM((ROW, 1, TOK), F32),
            pltpu.VMEM((24, TOK), F32),
            pltpu.VMEM((ROWS - 1, 24, TOK), F32),
            pltpu.VMEM((ROW, STATE, TOK), F32),
            pltpu.VMEM((PAIRS, STATE, TOK), F32),
            pltpu.VMEM((TOK, 1024), F32),
            pltpu.VMEM((TOK, 1024), F32),
            pltpu.VMEM((8, TOK), F32),
            pltpu.VMEM((TP, 8, TOK), F32),
            pltpu.VMEM((ROW, STATE, TOK), F32),
            pltpu.SemaphoreType.DMA((11,)),
            pltpu.SemaphoreType.DMA((2,)),
            pltpu.SemaphoreType.DMA((2, 2, 8)),
            pltpu.SemaphoreType.DMA((3,)),
            pltpu.SemaphoreType.DMA((3,)),
            pltpu.SemaphoreType.DMA((3,)),
            pltpu.SemaphoreType.DMA((3,)),
            pltpu.SemaphoreType.DMA((3,)),
            pltpu.SemaphoreType.DMA((3,)),
            pltpu.SemaphoreType.DMA((3,)),
            pltpu.SemaphoreType.DMA((3,)),
            pltpu.SemaphoreType.DMA((6,)),
            pltpu.SemaphoreType.DMA((6,)),
            pltpu.SemaphoreType.REGULAR((2,)),
        ],
        compiler_params=pltpu.CompilerParams(
            collective_id=0, has_side_effects=True, vmem_limit_bytes=48 << 20
        ),
    )(*[pltpu.with_memory_space_constraint(a, pltpu.HBM) for a in (
        queries, keys, values, mixer_input, gate, step_weight, state_weight.T, step_bias,
        decay_rate, skip_gain, norm_gain.reshape(1, -1),
    )])

    return pl.pallas_call(
        write_out,
        out_shape=shapes,
        in_specs=[pl.BlockSpec(memory_space=pltpu.VMEM)] * 2,
        out_specs=(hbm, hbm),
        scratch_shapes=[pltpu.SemaphoreType.DMA((2,))],
        compiler_params=pltpu.CompilerParams(vmem_limit_bytes=8 << 20),
    )(*results)


def solution(mesh):
    return jax.shard_map(
        per_device,
        mesh=mesh,
        in_specs=(P("ctx", "tp"),) * 5 + (P("tp", None),) * 2 + (P("tp"),) * 4,
        out_specs=(P("ctx", "tp"), P("ctx", "tp")),
        check_vma=False,
    )
```
